32 devices in a mesh: seq: 32 (over z, y, x, core), tp: 1.
Axes of the slice: x: 2, y: 2, z: 4, core: 2. Of those that a mesh axis runs over, the one named last changes fastest.
Arguments:
- queries: bfloat16 [4096, 4096], P('seq', 'tp'), may hold values from -128 to 128
- rotated_keys: bfloat16 [4096, 1024], P('seq', 'tp'), may hold values from -4.5 to 4.5
- values: bfloat16 [4096, 1024], P('seq', 'tp'), may hold values from -64 to 64
- decay_rates: float32 [64], P('tp'), may hold values from 2e-06 to 0.016
- decay_codes: int32 [4096, 64], P('seq', 'tp'), may hold values from 1 to 4096
- gate_input: bfloat16 [4096, 4096], P('seq', 'tp'), may hold values from -64 to 64
- norm_gain: float32 [4096], P('tp'), may hold values from 0.1 to 1.9
- bc_weight: bfloat16 [4096, 256], P('tp'), may hold values from -0.09375 to 0.09375
Outputs:
- first_pass: float32 [4096, 4096], P('seq', 'tp')
- second_pass: float32 [4096, 4096], P('seq', 'tp')
The draws below stay inside these ranges and needn't reach their ends.
All inputs are finite; a program needn't handle non-finite values.
Results may differ from the reference program's by a relative error of at most 0.017.
Values may be sent and summed in bfloat16 or wider, within the bound.
No kernel may reach another device: no remote copies, remote signals or barrier semaphores. Data moves between devices by JAX's collectives and lax.ppermute only.
A program may use at most 128 MiB of HBM per device.

```python
import math
import jax
import jax.numpy as jnp
from jax import lax

QUERY_HEADS = 32
KEY_VALUE_HEADS = 8
HEAD_SIZE = 128
SH = 64
SP = 64
NS = 128
WINDOW_LENGTH = 2048
STRETCH = 128
TOKENS_PER_SHARD = 128
SERIES_POSITIONS = 4096
WIDTH = 4096


def draw_decay_codes(key, part):
    tier_seed_handle, initial_seed_handle, spike_seed_handle = jax.random.split(jax.random.fold_in(key, 11), 3)
    block_total = SERIES_POSITIONS // TOKENS_PER_SHARD
    levels = jax.random.randint(tier_seed_handle, (block_total, 1, 1), 1, 5)
    raw_codes = jax.random.randint(initial_seed_handle, (block_total, TOKENS_PER_SHARD, SH), 0, 840)
    initial_integers = (raw_codes % (2 * levels) + 1).reshape(SERIES_POSITIONS, SH)
    spike_line_collection = jax.random.permutation(spike_seed_handle, SERIES_POSITIONS)[:3]
    spike_hits = jnp.zeros((SERIES_POSITIONS,), jnp.int32).at[spike_line_collection].set(1)
    return jnp.where(spike_hits[:, None] > 0, SERIES_POSITIONS, initial_integers).astype(jnp.int32)


def draw_decay_rates(key, part):
    slow_key, middle_key, fast_key, pick_key = jax.random.split(jax.random.fold_in(key, 23), 4)
    slow_rates = jax.random.uniform(slow_key, (SH,), jnp.float32, 0.3, 0.6) / (2.0 * SERIES_POSITIONS)
    middle_rates = jnp.exp(jax.random.uniform(middle_key, (SH,), jnp.float32, math.log(0.2), math.log(1.0))) / TOKENS_PER_SHARD
    middle_rates = jnp.minimum(middle_rates, 0.016)
    fast_rates = jnp.exp(jax.random.uniform(fast_key, (SH,), jnp.float32, math.log(0.008), math.log(0.016)))
    fast_share = 0.25
    middle_share = 0.25
    picker = jax.random.uniform(pick_key, (SH,), jnp.float32)
    chosen = jnp.where(picker < fast_share + middle_share, middle_rates, slow_rates)
    return jnp.where(picker < fast_share, fast_rates, chosen)


def shared_keys(key):
    initial_seed_handle = jax.random.fold_in(jax.random.fold_in(key, 41), 0)
    key_lookup_table = jnp.clip(jax.random.normal(initial_seed_handle, (SERIES_POSITIONS, KEY_VALUE_HEADS * HEAD_SIZE), jnp.float32), -4.5, 4.5)
    return key_lookup_table


def draw_rotated_keys(key, part):
    key_lookup_table = shared_keys(key)
    return key_lookup_table.astype(jnp.bfloat16)


def draw_queries(key, part):
    query_table = jnp.clip(jax.random.normal(jax.random.fold_in(key, 43), (SERIES_POSITIONS, QUERY_HEADS * HEAD_SIZE), jnp.float32), -4.5, 4.5)
    return jnp.clip(query_table, -128.0, 128.0).astype(jnp.bfloat16)


def noise_scaled(key, width_total, group_width):
    noise_key, column_key, row_key = jax.random.split(key, 3)
    noise_table = jnp.clip(jax.random.normal(noise_key, (SERIES_POSITIONS, width_total), jnp.float32), -4.5, 4.5)
    column_scale = jnp.exp(jax.random.uniform(column_key, (width_total,), jnp.float32, 0.0, math.log(2.0)))
    row_scale = jnp.exp(jax.random.uniform(row_key, (SERIES_POSITIONS, 1), jnp.float32, 0.0, math.log(2.0)))
    position = (jnp.arange(width_total) // group_width).astype(jnp.float32) / max(width_total // group_width - 1, 1)
    rising = 3.0 ** position
    return jnp.clip(noise_table * column_scale * row_scale * rising, -64.0, 64.0)


def draw_values(key, part):
    return noise_scaled(jax.random.fold_in(key, 53), KEY_VALUE_HEADS * HEAD_SIZE, HEAD_SIZE).astype(jnp.bfloat16)


def draw_gate_input(key, part):
    return noise_scaled(jax.random.fold_in(key, 59), WIDTH, SP).astype(jnp.bfloat16)


def noise(key, dims, scale, bound, kind=jnp.bfloat16):
    array = scale * jax.random.normal(key, dims, jnp.float32)
    return jnp.clip(array, min=-bound, max=bound).astype(kind)


def setup_inputs(seed: int = 0) -> dict:
    key_of = jax.random.split(jax.random.key(seed), 9)
    return {
        "queries": draw_queries(jax.random.fold_in(key_of[8], 71), 0),
        "rotated_keys": draw_rotated_keys(jax.random.fold_in(key_of[8], 71), 0),
        "values": draw_values(jax.random.fold_in(key_of[8], 71), 0),
        "decay_rates": draw_decay_rates(jax.random.fold_in(key_of[8], 71), 0),
        "decay_codes": draw_decay_codes(jax.random.fold_in(key_of[8], 71), 0),
        "gate_input": draw_gate_input(jax.random.fold_in(key_of[8], 71), 0),
        "norm_gain": jnp.clip(1.0 + 0.18 * jax.random.normal(key_of[6], (WIDTH,), jnp.float32), 0.1, 1.9),
        "bc_weight": noise(key_of[7], (WIDTH, 2 * NS), WIDTH ** -0.5, 0.09375),
    }


EPSILON = 1e-05

def attention(queries, rotated_keys, values):
    group_length = QUERY_HEADS // KEY_VALUE_HEADS
    score_scale = 1.0 / math.sqrt(HEAD_SIZE)
    padding_width = jnp.zeros((WINDOW_LENGTH, KEY_VALUE_HEADS * HEAD_SIZE), rotated_keys.dtype)
    extended_keys = jnp.concatenate([padding_width, rotated_keys], 0)
    extended_values = jnp.concatenate([padding_width, values], 0)
    offsets = jnp.arange(TOKENS_PER_SHARD, dtype=jnp.int32)
    key_offsets = jnp.arange(WINDOW_LENGTH + TOKENS_PER_SHARD, dtype=jnp.int32)

    def one_block(block_no):
        leading_row = (block_no * TOKENS_PER_SHARD).astype(jnp.int32)
        query_row_block = lax.dynamic_slice_in_dim(queries, leading_row, TOKENS_PER_SHARD, 0).reshape(TOKENS_PER_SHARD, KEY_VALUE_HEADS, group_length, HEAD_SIZE)
        key_row_block = lax.dynamic_slice_in_dim(extended_keys, leading_row, WINDOW_LENGTH + TOKENS_PER_SHARD, 0).reshape(WINDOW_LENGTH + TOKENS_PER_SHARD, KEY_VALUE_HEADS, HEAD_SIZE)
        value_row_block = lax.dynamic_slice_in_dim(extended_values, leading_row, WINDOW_LENGTH + TOKENS_PER_SHARD, 0).reshape(WINDOW_LENGTH + TOKENS_PER_SHARD, KEY_VALUE_HEADS, HEAD_SIZE)
        scores = jnp.einsum('tkgd,skd->kgts', query_row_block.astype(jnp.float32), key_row_block.astype(jnp.float32), precision=lax.Precision.HIGHEST) * score_scale
        query_pos = leading_row + offsets
        key_pos = leading_row - WINDOW_LENGTH + key_offsets
        allowed = (key_pos[None, :] <= query_pos[:, None]) & (key_pos[None, :] > query_pos[:, None] - WINDOW_LENGTH) & (key_pos[None, :] >= 0)
        scores = jnp.where(allowed[None, None], scores, -jnp.inf)
        row_max = lax.optimization_barrier(jnp.max(scores, axis=3, keepdims=True))
        exponent = jnp.exp(scores - row_max)
        probs = (exponent / lax.optimization_barrier(jnp.sum(exponent, axis=3, keepdims=True))).astype(jnp.bfloat16)
        mixed_rows = jnp.einsum('kgts,skd->tkgd', probs.astype(jnp.float32), value_row_block.astype(jnp.float32), precision=lax.Precision.HIGHEST)
        return mixed_rows.astype(jnp.bfloat16).reshape(TOKENS_PER_SHARD, QUERY_HEADS * HEAD_SIZE)
    blocks_out = lax.map(one_block, jnp.arange(SERIES_POSITIONS // TOKENS_PER_SHARD, dtype=jnp.int32))
    return blocks_out.reshape(SERIES_POSITIONS, QUERY_HEADS * HEAD_SIZE)

def core(inputs, decay_rates, decay_codes, gate_input, norm_gain, bc_weight):
    as_float = inputs.astype(jnp.float32)
    spread = jnp.sqrt(lax.optimization_barrier(jnp.mean(as_float * as_float, axis=1, keepdims=True)) + EPSILON)
    normed = (as_float / spread).astype(jnp.bfloat16)
    projected = (jnp.dot(inputs, bc_weight, preferred_element_type=jnp.float32) / spread).astype(jnp.bfloat16)
    stretch_count = SERIES_POSITIONS // STRETCH
    x_stretches = normed.reshape(stretch_count, STRETCH, SH, SP)
    b_stretches = projected[:, :NS].reshape(stretch_count, STRETCH, NS)
    c_stretches = projected[:, NS:].reshape(stretch_count, STRETCH, NS)
    code_stretches = decay_codes.reshape(stretch_count, STRETCH, SH)
    lower_mask = (jnp.arange(STRETCH)[:, None] >= jnp.arange(STRETCH)[None, :])[:, :, None]

    def advance(state, pieces):
        x_block, b_block, c_block, code_block = pieces
        ell = -decay_rates[None, :] * jnp.cumsum(code_block, axis=0, dtype=jnp.int32).astype(jnp.float32)
        gram_matrix = jnp.dot(c_block, b_block.T, preferred_element_type=jnp.float32)
        decay_gaps = jnp.where(lower_mask, ell[:, None, :] - ell[None, :, :], 0.0)
        mixing = jnp.where(lower_mask, gram_matrix[:, :, None] * jnp.exp(decay_gaps), 0.0).astype(jnp.bfloat16)
        y_local = jnp.einsum('tsh,shp->thp', mixing.astype(jnp.float32), x_block.astype(jnp.float32), precision=lax.Precision.HIGHEST)
        tail_decay = jnp.exp(ell[-1][None, :] - ell)
        b_weighted = (b_block.astype(jnp.float32)[:, None, :] * tail_decay[:, :, None]).astype(jnp.bfloat16)
        contrib = jnp.einsum('shn,shp->hnp', b_weighted.astype(jnp.float32), x_block.astype(jnp.float32), precision=lax.Precision.HIGHEST)
        c_weighted = c_block.astype(jnp.float32)[:, None, :] * jnp.exp(ell)[:, :, None]
        y_carried = jnp.einsum('thn,hnp->thp', c_weighted, state, precision=lax.Precision.HIGHEST)
        new_state = jnp.exp(ell[-1])[:, None, None] * state + contrib
        return (new_state, y_local + y_carried)
    start_state = jnp.zeros((SH, NS, SP), jnp.float32)
    final_state, y_blocks = lax.scan(advance, start_state, (x_stretches, b_stretches, c_stretches, code_stretches))
    y_all = y_blocks.reshape(SERIES_POSITIONS, SH * SP)
    gated_out = y_all * jax.nn.silu(gate_input.astype(jnp.float32))
    out_scale = jnp.sqrt(lax.optimization_barrier(jnp.mean(gated_out * gated_out, axis=1, keepdims=True)) + EPSILON)
    return gated_out / out_scale * norm_gain

def reference(queries, rotated_keys, values, decay_rates, decay_codes, gate_input, norm_gain, bc_weight):
    attended = attention(queries, rotated_keys, values)
    first_pass = core(attended, decay_rates, decay_codes, gate_input, norm_gain, bc_weight)
    pass_input = first_pass.astype(jnp.bfloat16)
    second_pass = core(pass_input, decay_rates, decay_codes, gate_input, norm_gain, bc_weight)
    return (first_pass, second_pass)
```

```python
import functools
import math

import jax
import jax.numpy as jnp
from jax import lax
from jax.experimental import pallas as pl
from jax.experimental.pallas import tpu as pltpu
from jax.sharding import Mesh
from jax.sharding import PartitionSpec as P

QUERY_HEADS = 32
KEY_VALUE_HEADS = 8
HEAD_SIZE = 128
SH = 64
SP = 64
NS = 128
WINDOW_LENGTH = 2048
STRETCH = 128


EPSILON = 1e-05


def shifted(block, axis, distance):
    devices = range(lax.axis_size(axis))
    route = [(i - distance, i) for i in devices if i - distance in devices]
    return lax.ppermute(block, axis, route)


def prefix(x, axis, combine, identity):
    peers, index = (lax.axis_size(axis), lax.axis_index(axis))
    everything = jax.tree.map(lambda part: lax.all_gather(part, axis), x)
    start = jax.tree.map(
        lambda part, zero: jnp.broadcast_to(jnp.asarray(zero, part.dtype), part.shape), x, identity
    )

    def step(k, before):
        reached = k < index
        new = combine(before, jax.tree.map(lambda part: part[k], everything))
        return jax.tree.map(lambda a, b: jnp.where(reached, a, b), new, before)

    return lax.fori_loop(0, peers, step, start)


def combine_states(earlier, later):
    return (earlier[0] * later[0], later[0][..., None, None] * earlier[1] + later[1])


def attention(queries, rotated_keys, values):
    tok_rows = queries.shape[0]
    seq_index = lax.axis_index("seq")
    reach = WINDOW_LENGTH // tok_rows
    kv_local = rotated_keys.shape[1] // HEAD_SIZE
    group_length = QUERY_HEADS // KEY_VALUE_HEADS
    paired = jnp.stack([rotated_keys, values], 0)
    moving = paired
    arrived = []
    for counter in range(reach):
        moving = shifted(moving, "seq", 1)
        arrived.append(moving)
    kv_blocks = arrived[::-1]
    window_kv = jnp.concatenate(kv_blocks + [paired], 1)
    grouped = queries.reshape(tok_rows, kv_local, group_length, HEAD_SIZE)
    score_scale = 1.0 / math.sqrt(HEAD_SIZE)
    query_pos = seq_index * tok_rows + jnp.arange(tok_rows, dtype=jnp.int32)
    base_pos = (seq_index - reach) * tok_rows

    def block_scores(key_block):
        key_row_block = lax.dynamic_slice_in_dim(
            window_kv[0], key_block * tok_rows, tok_rows, 0
        ).reshape(tok_rows, kv_local, HEAD_SIZE)
        scores = (
            jnp.einsum("tkgd,skd->kgts", grouped, key_row_block, preferred_element_type=jnp.float32)
            * score_scale
        )
        key_pos = base_pos + key_block * tok_rows + jnp.arange(tok_rows, dtype=jnp.int32)
        allowed = (
            (key_pos[None, :] <= query_pos[:, None])
            & (key_pos[None, :] > query_pos[:, None] - WINDOW_LENGTH)
            & (key_pos[None, :] >= 0)
        )
        return jnp.where(allowed[None, None], scores, -jnp.inf)

    def visit_order(counter):
        return (counter + reach) % (reach + 1)

    def totals(counter, running):
        row_max, row_sum = running
        scores = block_scores(visit_order(counter))
        new_max = jnp.maximum(row_max, jnp.max(scores, axis=3))
        rescale = jnp.exp(row_max - new_max)
        row_sum = row_sum * rescale + jnp.sum(jnp.exp(scores - new_max[..., None]), axis=3)
        return (new_max, row_sum)

    max_init = jnp.full((kv_local, group_length, tok_rows), -jnp.inf, jnp.float32)
    row_max, row_sum = lax.fori_loop(0, reach + 1, totals, (max_init, jnp.zeros_like(max_init)))

    def weighted(counter, accumulated):
        key_block = visit_order(counter)
        scores = block_scores(key_block)
        value_row_block = lax.dynamic_slice_in_dim(
            window_kv[1], key_block * tok_rows, tok_rows, 0
        ).reshape(tok_rows, kv_local, HEAD_SIZE)
        probs = (jnp.exp(scores - row_max[..., None]) / row_sum[..., None]).astype(jnp.bfloat16)
        return accumulated + jnp.einsum(
            "kgts,skd->kgtd", probs, value_row_block, preferred_element_type=jnp.float32
        )

    acc_init = jnp.zeros((kv_local, group_length, tok_rows, HEAD_SIZE), jnp.float32)
    accumulated = lax.fori_loop(0, reach + 1, weighted, acc_init)
    mixed_rows = jnp.transpose(accumulated, (2, 0, 1, 3))
    return mixed_rows.astype(jnp.bfloat16).reshape(tok_rows, kv_local * group_length * HEAD_SIZE)


def core(inputs, decay_rates, decay_codes, gate_input, norm_gain, bc_weight):
    tok_rows = inputs.shape[0]
    head_count = decay_rates.shape[0]
    channels = SH * SP
    as_float = inputs.astype(jnp.float32)
    own_squares = jnp.sum(as_float * as_float, axis=1)
    partial_value = jnp.dot(inputs, bc_weight, preferred_element_type=jnp.float32)
    total_squares = lax.psum(own_squares, "tp")
    spread = jnp.sqrt(total_squares / channels + EPSILON)[:, None]
    projected = lax.psum(partial_value / spread, "tp")
    normed = (as_float / spread).astype(jnp.bfloat16)
    projected = projected.astype(jnp.bfloat16)
    stretch_count = tok_rows // STRETCH
    x_stretches = normed.reshape(stretch_count, STRETCH, head_count, SP)
    b_stretches = projected[:, :NS].reshape(stretch_count, STRETCH, NS)
    c_stretches = projected[:, NS:].reshape(stretch_count, STRETCH, NS)
    summed_codes = jnp.cumsum(
        decay_codes.reshape(stretch_count, STRETCH, head_count), axis=1, dtype=jnp.int32
    )
    log_decay = -decay_rates * summed_codes.astype(jnp.float32)
    decay_by_head = jnp.transpose(log_decay, (0, 2, 1))
    gram_matrix = jnp.einsum(
        "ctn,csn->cts", c_stretches, b_stretches, preferred_element_type=jnp.float32
    )
    lower_mask = jnp.arange(STRETCH)[:, None] >= jnp.arange(STRETCH)[None, :]
    decay_gaps = jnp.where(
        lower_mask, decay_by_head[..., :, None] - decay_by_head[..., None, :], 0.0
    )
    mixing = jnp.where(lower_mask, gram_matrix[:, None] * jnp.exp(decay_gaps), 0.0).astype(
        jnp.bfloat16
    )
    y_local = jnp.einsum("chts,cshp->cthp", mixing, x_stretches, preferred_element_type=jnp.float32)
    tail_decay = jnp.exp(decay_by_head[..., -1:] - decay_by_head)
    b_weighted = (b_stretches.astype(jnp.float32)[:, None] * tail_decay[..., None]).astype(
        jnp.bfloat16
    )
    contrib = jnp.einsum(
        "chsn,cshp->chnp", b_weighted, x_stretches, preferred_element_type=jnp.float32
    )
    stretch_decay = jnp.exp(decay_by_head[..., -1])
    carried_decay = jnp.ones((head_count,), jnp.float32)
    carried_state = jnp.zeros((head_count, NS, SP), jnp.float32)
    carried_state = stretch_decay[0][:, None, None] * carried_state + contrib[0]
    carried_decay = carried_decay * stretch_decay[0]
    unused_decay, entering = prefix(
        (carried_decay, carried_state),
        "seq",
        combine_states,
        (jnp.ones_like(carried_decay), jnp.zeros_like(carried_state)),
    )
    states = [entering]
    stacked = jnp.stack(states, 0)
    c_weighted = c_stretches.astype(jnp.float32)[:, None] * jnp.exp(decay_by_head)[..., None]
    y_carried = jnp.einsum(
        "chtn,chnp->cthp",
        c_weighted,
        stacked,
        precision=lax.Precision.HIGHEST,
        preferred_element_type=jnp.float32,
    )
    outputs = (y_local + y_carried).reshape(tok_rows, head_count * SP)
    gated_out = outputs * jax.nn.silu(gate_input.astype(jnp.float32))
    gate_squares = lax.psum(jnp.sum(gated_out * gated_out, axis=1), "tp")
    out_scale = jnp.sqrt(gate_squares / channels + EPSILON)[:, None]
    return gated_out / out_scale * norm_gain


def on_device(
    queries, rotated_keys, values, decay_rates, decay_codes, gate_input, norm_gain, bc_weight
):
    attended = attention(queries, rotated_keys, values)
    first_pass = core(attended, decay_rates, decay_codes, gate_input, norm_gain, bc_weight)
    pass_input = first_pass.astype(jnp.bfloat16)
    second_pass = core(pass_input, decay_rates, decay_codes, gate_input, norm_gain, bc_weight)
    return (first_pass, second_pass)


F32 = jnp.float32
BF16 = jnp.bfloat16
LANES = 128
INNER = (((1,), (1,)), ((), ()))
VMEM_BYTES = 60 * 1024 * 1024


def dot(a, b, dims=(((1,), (0,)), ((), ()))):
    return lax.dot_general(a, b, dims, preferred_element_type=F32)


def lane_select(low, high):
    lane = lax.broadcasted_iota(jnp.int32, (1, LANES), 1)
    return jnp.where(lane < SP, low, high)


def split_rows(*rows):
    which = lax.broadcasted_iota(jnp.int32, (16, LANES), 0)
    tile = jnp.zeros((16, LANES), F32)
    for i, row in enumerate(rows):
        for n in range(3):
            piece = row.astype(BF16).astype(F32)
            tile = jnp.where(which == 3 * i + n, piece, tile)
            row = row - piece
    return jnp.concatenate([tile, jnp.zeros_like(tile)], 1).astype(BF16)


def joined_row(proj_ref, i):
    pieces = proj_ref[0, LANES:, :LANES].astype(F32)
    return pieces[3 * i : 3 * i + 1] + pieces[3 * i + 1 : 3 * i + 2] + pieces[3 * i + 2 : 3 * i + 3]


def column(row):
    return jnp.broadcast_to(row, (LANES, LANES)).T


def pack_kv_kernel(k_ref, v_ref, out_ref):
    out_ref[0, :LANES, :] = k_ref[...]
    out_ref[0, LANES:, :] = v_ref[...]


def pack_kernel(q_ref, gate_ref, codes_ref, out_ref):
    heads = q_ref.shape[1] // LANES
    for h in range(heads):
        cols = pl.ds(h * LANES, LANES)
        out_ref[0, pl.ds(h * LANES, LANES), :] = q_ref[:, cols]
        out_ref[0, pl.ds((heads + h) * LANES, LANES), :] = gate_ref[:, cols]
    out_ref[0, pl.ds(2 * heads * LANES, 16), :] = codes_ref[0]


def attend_kernel(
    place_ref, q_ref, ko_ref, vo_ref, k1_ref, v1_ref, k2_ref, v2_ref, bc_ref, x_ref, part_ref, s_ref
):
    j = pl.program_id(0)
    plane = place_ref[0]
    blocks = ko_ref.shape[0]
    rows = q_ref.shape[1]
    q = q_ref[0]
    bias1 = jnp.where(plane >= 1, 0.0, -jnp.inf).astype(F32)
    bias2 = jnp.where(plane >= 2, 0.0, -jnp.inf).astype(F32)
    lane = lax.broadcasted_iota(jnp.int32, (1, 2 * LANES), 1)
    t_pos = lax.broadcasted_iota(jnp.int32, (rows, LANES), 0) % LANES
    s_pos = lax.broadcasted_iota(jnp.int32, (rows, LANES), 1)
    causal = s_pos <= t_pos
    half = blocks // 2

    def mixed(i, own_ref, far_ref):
        return jnp.where(i < j, own_ref[i], far_ref[i + 1])

    top = None
    for i in range(2 * half):
        if i < half:
            keys = k1_ref[2 * i : 2 * i + 2].reshape(2 * LANES, HEAD_SIZE)
            s = dot(q, keys, INNER) + bias1
        else:
            a = 2 * (i - half)
            first = mixed(a, ko_ref, k2_ref)
            bias_a = jnp.where(a < j, 0.0, bias2)
            if i < 2 * half - 1:
                keys = jnp.concatenate([first, mixed(a + 1, ko_ref, k2_ref)], 0)
                bias_b = jnp.where(a + 1 < j, 0.0, bias2)
                s = dot(q, keys, INNER) + jnp.where(lane < LANES, bias_a, bias_b)
            else:
                keys = jnp.concatenate([first, ko_ref[j]], 0)
                s = dot(q, keys, INNER)
                edge = dot(q, k2_ref[j], INNER) + bias2
                s = jnp.concatenate(
                    [s[:, :LANES] + bias_a, jnp.where(causal, s[:, LANES:], edge)], 1
                )
        s_ref[i] = s
        high = jnp.maximum(s[:, :LANES], s[:, LANES:])
        top = high if top is None else jnp.maximum(top, high)
    factor = math.log2(math.e) / math.sqrt(HEAD_SIZE)
    top = jnp.max(top, axis=1, keepdims=True) * factor
    weight = jnp.zeros((rows, LANES), F32)
    for i in range(2 * half):
        p = jnp.exp2(s_ref[i] * factor - top)
        s_ref[i] = p
        weight += p[:, :LANES] + p[:, LANES:]
    weight = 1.0 / jnp.sum(weight, axis=1, keepdims=True)
    total = jnp.zeros((rows, HEAD_SIZE), F32)
    for i in range(2 * half):
        p = (s_ref[i] * weight).astype(BF16)
        if i < half:
            vals = v1_ref[2 * i : 2 * i + 2].reshape(2 * LANES, HEAD_SIZE)
        else:
            a = 2 * (i - half)
            first = mixed(a, vo_ref, v2_ref)
            if i < 2 * half - 1:
                vals = jnp.concatenate([first, mixed(a + 1, vo_ref, v2_ref)], 0)
            else:
                last = p[:, LANES:]
                zero = jnp.zeros_like(last)
                far = jnp.where(causal, zero, last)
                p = jnp.concatenate([p[:, :LANES], jnp.where(causal, last, zero)], 1)
                vals = jnp.concatenate([first, vo_ref[j]], 0)
                total += dot(far, v2_ref[j])
        total += dot(p, vals)
    x = total.astype(BF16)
    x_ref[0] = x
    heads = rows // LANES
    part = jnp.zeros((LANES, 2 * NS), F32)
    squares = jnp.zeros((LANES, LANES), F32)
    for h in range(heads):
        piece = x[h * LANES : (h + 1) * LANES]
        part += dot(piece, bc_ref[pl.ds(h * LANES, LANES), :])
        wide = piece.astype(F32)
        squares += wide * wide
    high = squares.astype(BF16)
    low = (squares - high.astype(F32)).astype(BF16)
    row_ones = jnp.ones((16, LANES), BF16)
    row = dot(row_ones, high, INNER) + dot(row_ones, low, INNER)
    part_ref[0, :LANES, :] = part
    part_ref[0, LANES:, :LANES] = row[:8]
    part_ref[0, LANES:, LANES:] = jnp.zeros_like(row[:8])


def project_kernel(channels, part_ref, out_ref):
    total = part_ref[0]
    for i in range(1, part_ref.shape[0]):
        total += part_ref[i]
    inverse = 1.0 / jnp.sqrt(total[LANES : LANES + 1, :LANES] / channels + EPSILON)
    scale = column(inverse)
    out_ref[:LANES, :NS] = (total[:LANES, :NS] * scale).astype(BF16)
    out_ref[:LANES, NS:] = (total[:LANES, NS:] * scale).astype(BF16)
    out_ref[LANES:, :] = split_rows(inverse)


def code_sums(codes_ref):
    u = lax.broadcasted_iota(jnp.int32, (LANES, LANES), 0)
    t = lax.broadcasted_iota(jnp.int32, (LANES, LANES), 1)
    upper = jnp.where(u <= t, 1.0, 0.0).astype(BF16)
    sums = dot(codes_ref[0], upper)
    return sums[:8] * 128.0 + sums[8:]


def columns_of(by_row):
    pad = jnp.zeros((LANES - by_row.shape[0], LANES), F32)
    return jnp.concatenate([by_row, pad], 0).T


def states_kernel(with_gain, place_ref, x_ref, proj_ref, codes_ref, rates_ref, *rest):
    if with_gain:
        gain_ref, *rest = rest
    normed_ref, enter_ref, end_ref, decay_ref, state_ref, count_ref = rest
    k = pl.program_id(0)

    @pl.when(k == 0)
    def _():
        state_ref[...] = jnp.zeros_like(state_ref)
        count_ref[...] = jnp.zeros_like(count_ref)

    sums = code_sums(codes_ref)
    last = sums[:, LANES - 1 :]
    weights = jnp.exp(-rates_ref[0] * (last - sums))
    block_decay = jnp.exp(-rates_ref[0] * last)
    count_ref[...] += jnp.broadcast_to(last, count_ref.shape)
    b_across = proj_ref[0, :LANES, :NS].astype(F32).T
    inverse = column(joined_row(proj_ref, 0))
    if with_gain:
        out_inverse = column(joined_row(proj_ref, 1))
    for pair in range(x_ref.shape[1] // LANES):
        rows = pl.ds(pair * LANES, LANES)
        x = x_ref[0, rows, :].astype(F32)
        if with_gain:
            x = x * out_inverse * gain_ref[0, pair : pair + 1, :]
            x = x.astype(BF16).astype(F32)
        x = (x * inverse).astype(BF16)
        normed_ref[0, rows, :] = x
        h = 2 * pair
        b = jnp.concatenate(
            [b_across * weights[h : h + 1], b_across * weights[h + 1 : h + 2]], 0
        ).astype(BF16)
        both = dot(b, x)
        contrib = lane_select(both[:NS], both[NS:])
        state = state_ref[rows, :]
        enter_ref[0, rows, :] = state
        decay = lane_select(block_decay[h : h + 1], block_decay[h + 1 : h + 2])
        state_ref[rows, :] = decay * state + contrib

    @pl.when(k == pl.num_programs(0) - 1)
    def _():
        end_ref[...] = state_ref[...].astype(BF16)
        whole = jnp.exp(-rates_ref[0] * count_ref[...])
        for pair in range(x_ref.shape[1] // LANES):
            decay_ref[pair : pair + 1, :] = lane_select(
                whole[2 * pair : 2 * pair + 1], whole[2 * pair + 1 : 2 * pair + 2]
            )
        decay_ref[4:, :] = jnp.zeros((4, LANES), F32)


def local_kernel(place_ref, x_ref, proj_ref, codes_ref, rates_ref, enter_ref, y_ref):
    ell = -rates_ref[0] * code_sums(codes_ref)
    ell_col = columns_of(ell)
    grown = jnp.exp(ell_col)
    b = proj_ref[0, :LANES, :NS]
    c = proj_ref[0, :LANES, NS:]
    gram = dot(c, b, INNER)
    c = c.astype(F32)
    t = lax.broadcasted_iota(jnp.int32, (LANES, LANES), 0)
    s = lax.broadcasted_iota(jnp.int32, (LANES, LANES), 1)
    lower = t >= s
    lane = lax.broadcasted_iota(jnp.int32, (LANES, LANES), 1)
    for pair in range(x_ref.shape[1] // LANES):
        mixes, highs, lows = [], [], []
        for h in (2 * pair, 2 * pair + 1):
            gap = jnp.where(lower, ell_col[:, h : h + 1] - ell[h : h + 1], -jnp.inf)
            mixes.append((gram * jnp.exp(gap)).astype(BF16))
            carry = c * grown[:, h : h + 1]
            high = carry.astype(BF16)
            highs.append(high)
            lows.append((carry - high.astype(F32)).astype(BF16))
        x = x_ref[0, pl.ds(pair * LANES, LANES), :]
        state = enter_ref[0, pl.ds(pair * NS, NS), :]
        high = state.astype(BF16)
        low = (state - high.astype(F32)).astype(BF16)
        zero = jnp.zeros_like(x)

        def halves(v):
            return [jnp.where(lane < SP, v, zero), jnp.where(lane < SP, zero, v)]

        right = jnp.concatenate(halves(x) + halves(high) + halves(low) + halves(high), 0)
        left = jnp.concatenate(mixes + highs + highs + lows, 1)
        y_ref[0, pl.ds(pair * LANES, LANES), :] = dot(left, right)


def gated_kernel(planes, place_ref, y_ref, gate_ref, proj_ref, codes_ref, rates_ref, *rest):
    states, decays = rest[: planes - 1], rest[planes - 1 : 2 * planes - 3]
    out_ref, full_ref, count_ref = rest[2 * planes - 3 :]
    k = pl.program_id(0)

    @pl.when(k == 0)
    def _():
        count_ref[...] = jnp.zeros_like(count_ref)

    sums = code_sums(codes_ref)
    ell = -rates_ref[0] * (sums + count_ref[...])
    count_ref[...] += jnp.broadcast_to(sums[:, LANES - 1 :], count_ref.shape)
    grown = columns_of(jnp.exp(ell))
    c = proj_ref[0, :LANES, NS:].astype(F32)
    lane = lax.broadcasted_iota(jnp.int32, (LANES, LANES), 1)
    for pair in range(y_ref.shape[1] // LANES):
        rows = pl.ds(pair * LANES, LANES)
        state = states[-1][rows, :].astype(F32)
        for i in range(planes - 3, -1, -1):
            state = states[i][rows, :].astype(F32) + decays[i][pair : pair + 1, :] * state
        state = state.astype(BF16)
        zero = jnp.zeros_like(state)
        right = jnp.concatenate(
            [jnp.where(lane < SP, state, zero), jnp.where(lane < SP, zero, state)], 0
        )
        h = 2 * pair
        left = jnp.concatenate([c * grown[:, h : h + 1], c * grown[:, h + 1 : h + 2]], 1)
        y = y_ref[0, rows, :] + dot(left.astype(BF16), right)
        gate = gate_ref[0, rows, :].astype(F32)
        y = y * (gate / (1.0 + jnp.exp(-gate)))
        out_ref[0, rows, :] = y.astype(BF16)
        full_ref[0, rows, :] = y


def finish_kernel(channels, with_proj, g_ref, gain_ref, *rest):
    if with_proj:
        bc_ref, out_ref, proj_ref = rest
    else:
        (out_ref,) = rest
    parts, wide = g_ref.shape[0], g_ref.shape[1] // LANES
    squares = jnp.zeros((LANES, LANES), F32)
    for p in range(parts):
        for i in range(wide):
            g = g_ref[p, i * LANES : (i + 1) * LANES, :].astype(F32)
            squares += g * g
    inverse = 1.0 / jnp.sqrt(jnp.sum(squares, 1, keepdims=True) / channels + EPSILON)
    scaled = jnp.zeros((LANES, LANES), F32)
    proj = jnp.zeros((LANES, 2 * NS), F32)
    for p in range(parts):
        for i in range(wide):
            n = p * wide + i
            g = g_ref[p, i * LANES : (i + 1) * LANES, :].astype(F32)
            out = g * inverse * gain_ref[n : n + 1, :]
            out_ref[:, n * LANES : (n + 1) * LANES] = out
            if with_proj:
                x = out.astype(BF16)
                proj += dot(x, bc_ref[n * LANES : (n + 1) * LANES, :])
                x = x.astype(F32)
                scaled += x * x
    if with_proj:
        mean = jnp.sum(scaled, 1, keepdims=True) / channels
        both = 1.0 / jnp.sqrt(mean + EPSILON)
        proj_ref[:LANES, :] = (proj * both).astype(BF16)
        wide = jnp.broadcast_to(both, (LANES, LANES)).T
        proj_ref[LANES:, :] = split_rows(wide[:1], jnp.broadcast_to(inverse, wide.shape).T[:1])


def params(**kw):
    return pltpu.CompilerParams(vmem_limit_bytes=VMEM_BYTES, **kw)


def cost(flops, nbytes, exps=0):
    return pl.CostEstimate(flops=flops, bytes_accessed=nbytes, transcendentals=exps)


def whole_block(shape):
    return pl.BlockSpec(shape, lambda *_: (0,) * len(shape))


def head_sharded(
    planes, queries, rotated_keys, values, decay_rates, decay_codes, gate_input, norm_gain, bc_weight
):
    tokens, channels = queries.shape
    peers = lax.axis_size("peer")
    wide = channels // peers
    pairs = wide // LANES
    place = jnp.stack([lax.axis_index("plane"), lax.axis_index("peer")]).astype(jnp.int32)

    def moved(x, distance):
        return lax.ppermute(x, "plane", [(i, i + distance) for i in range(planes - distance)])

    kv = pl.pallas_call(
        pack_kv_kernel,
        grid=(peers,),
        in_specs=[pl.BlockSpec((tokens, HEAD_SIZE), lambda p: (0, p))] * 2,
        out_specs=pl.BlockSpec((1, 2 * tokens, HEAD_SIZE), lambda p: (p, 0, 0)),
        out_shape=jax.ShapeDtypeStruct((peers, 2 * tokens, HEAD_SIZE), BF16),
        name="pack_kv",
    )(rotated_keys, values)
    kv_own = lax.all_to_all(kv, "peer", 0, 0)
    kv_one = moved(kv_own, 1)
    kv_two = moved(kv_one, 1)

    coded = jnp.stack([decay_codes >> 7, decay_codes & 127], 0).astype(BF16)
    heads = decay_codes.shape[1] // peers
    coded = jnp.transpose(coded.reshape(2, tokens, peers, heads), (2, 0, 3, 1))
    coded = coded.reshape(peers, 2 * heads, tokens)
    q_rows = 2 * wide + 2 * heads
    packed = pl.pallas_call(
        pack_kernel,
        grid=(peers,),
        in_specs=[
            pl.BlockSpec((tokens, wide), lambda p: (0, p)),
            pl.BlockSpec((tokens, wide), lambda p: (0, p)),
            pl.BlockSpec((1, 2 * heads, tokens), lambda p: (p, 0, 0)),
        ],
        out_specs=pl.BlockSpec((1, q_rows, LANES), lambda p: (p, 0, 0)),
        out_shape=jax.ShapeDtypeStruct((peers, q_rows, LANES), BF16),
        name="pack_queries",
    )(queries, gate_input, coded)
    arrived = lax.all_to_all(packed, "peer", 0, 0)

    def keys_spec(which):
        return pl.BlockSpec((peers, tokens, HEAD_SIZE), lambda j, s: (0, which, 0))

    def block(rows, which=0, lanes=LANES):
        return pl.BlockSpec((1, rows, lanes), lambda j, s: (j, which, 0))

    proj_rows = tokens + 16
    attended, partial = pl.pallas_call(
        attend_kernel,
        grid_spec=pltpu.PrefetchScalarGridSpec(
            num_scalar_prefetch=1,
            grid=(peers,),
            in_specs=[block(wide)]
            + [keys_spec(0), keys_spec(1)] * 3
            + [pl.BlockSpec((wide, 2 * NS), lambda j, s: (s[1], 0))],
            out_specs=[block(wide), block(tokens + 8, 0, 2 * NS)],
            scratch_shapes=[pltpu.VMEM((peers, wide, 2 * tokens), F32)],
        ),
        out_shape=[
            jax.ShapeDtypeStruct((peers, wide, LANES), BF16),
            jax.ShapeDtypeStruct((peers, tokens + 8, 2 * NS), F32),
        ],
        compiler_params=params(),
        cost_estimate=cost(5 * 10**9, 4 * 10**6, 9 * 10**6),
        name="attend",
    )(place, arrived, kv_own, kv_own, kv_one, kv_one, kv_two, kv_two, bc_weight)

    shares = lax.all_to_all(partial, "peer", 0, 0)
    proj = pl.pallas_call(
        functools.partial(project_kernel, channels),
        in_specs=[whole_block((peers, tokens + 8, 2 * NS))],
        out_specs=whole_block((proj_rows, 2 * NS)),
        out_shape=jax.ShapeDtypeStruct((proj_rows, 2 * NS), BF16),
        name="project",
    )(shares)

    rates = jnp.broadcast_to(decay_rates.reshape(peers, heads, 1), (peers, heads, LANES))
    gains = norm_gain.reshape(peers, pairs, LANES)
    rates_spec = pl.BlockSpec((1, heads, LANES), lambda j, s: (s[1], 0, 0))
    gains_spec = pl.BlockSpec((1, pairs, LANES), lambda j, s: (s[1], 0, 0))
    codes_spec = block(2 * heads, 2 * wide // (2 * heads))
    proj_spec = block(proj_rows, 0, 2 * NS)

    def ssd(x, projected, with_gain, decays):
        common = [block(wide), proj_spec, codes_spec, rates_spec]
        operands = [x, projected, arrived, rates]
        if with_gain:
            common = common + [gains_spec]
            operands = operands + [gains]
        normed, entering, end, decay = pl.pallas_call(
            functools.partial(states_kernel, with_gain),
            grid_spec=pltpu.PrefetchScalarGridSpec(
                num_scalar_prefetch=1,
                grid=(peers,),
                in_specs=common,
                out_specs=[
                    block(wide),
                    block(wide),
                    pl.BlockSpec((wide, LANES), lambda j, s: (0, 0)),
                    pl.BlockSpec((8, LANES), lambda j, s: (0, 0)),
                ],
                scratch_shapes=[pltpu.VMEM((wide, LANES), F32), pltpu.VMEM((heads, LANES), F32)],
            ),
            out_shape=[
                jax.ShapeDtypeStruct((peers, wide, LANES), BF16),
                jax.ShapeDtypeStruct((peers, wide, LANES), F32),
                jax.ShapeDtypeStruct((wide, LANES), BF16),
                jax.ShapeDtypeStruct((8, LANES), F32),
            ],
            compiler_params=params(),
            cost_estimate=cost(10**9, 4 * 10**6),
            name="states",
        )(place, *operands)
        earlier = [moved(end, i) for i in range(1, planes)]
        if decays is None:
            decays = [moved(decay, i) for i in range(1, planes - 1)]
        y = pl.pallas_call(
            local_kernel,
            grid_spec=pltpu.PrefetchScalarGridSpec(
                num_scalar_prefetch=1,
                grid=(peers,),
                in_specs=[block(wide), proj_spec, codes_spec, rates_spec, block(wide)],
                out_specs=block(wide),
            ),
            out_shape=jax.ShapeDtypeStruct((peers, wide, LANES), F32),
            compiler_params=params(),
            cost_estimate=cost(2 * 10**9, 5 * 10**6, 10**6),
            name="local",
        )(place, normed, projected, arrived, rates, entering)
        gated, full = pl.pallas_call(
            functools.partial(gated_kernel, planes),
            grid_spec=pltpu.PrefetchScalarGridSpec(
                num_scalar_prefetch=1,
                grid=(peers,),
                in_specs=[block(wide), block(wide, 1), proj_spec, codes_spec, rates_spec]
                + [pl.BlockSpec((wide, LANES), lambda j, s: (0, 0))] * (planes - 1)
                + [pl.BlockSpec((8, LANES), lambda j, s: (0, 0))] * (planes - 2),
                out_specs=[block(wide), block(wide)],
                scratch_shapes=[pltpu.VMEM((heads, LANES), F32)],
            ),
            out_shape=[
                jax.ShapeDtypeStruct((peers, wide, LANES), BF16),
                jax.ShapeDtypeStruct((peers, wide, LANES), F32),
            ],
            compiler_params=params(),
            cost_estimate=cost(10**9, 5 * 10**6, 10**6),
            name="gated",
        )(place, y, arrived, projected, arrived, rates, *earlier, *decays)
        return gated, full, decays

    gain_rows = norm_gain.reshape(channels // LANES, LANES)
    gathered = (peers, wide, LANES)

    projected = lax.all_gather(proj, "peer")
    gated, full, decays = ssd(attended, projected, False, None)
    first, proj = pl.pallas_call(
        functools.partial(finish_kernel, channels, True),
        in_specs=[
            whole_block(gathered),
            whole_block(gain_rows.shape),
            whole_block((channels, 2 * NS)),
        ],
        out_specs=[whole_block((tokens, channels)), whole_block((proj_rows, 2 * NS))],
        out_shape=[
            jax.ShapeDtypeStruct((tokens, channels), F32),
            jax.ShapeDtypeStruct((proj_rows, 2 * NS), BF16),
        ],
        compiler_params=params(),
        name="finish_first",
    )(lax.all_to_all(gated, "peer", 0, 0), gain_rows, bc_weight)
    projected = lax.all_gather(proj, "peer")
    gated, _, _ = ssd(full, projected, True, decays)
    second = pl.pallas_call(
        functools.partial(finish_kernel, channels, False),
        in_specs=[whole_block(gathered), whole_block(gain_rows.shape)],
        out_specs=whole_block((tokens, channels)),
        out_shape=jax.ShapeDtypeStruct((tokens, channels), F32),
        compiler_params=params(),
        name="finish_second",
    )(lax.all_to_all(gated, "peer", 0, 0), gain_rows)
    return first, second


def solution(mesh):
    seq, tp = mesh.shape["seq"], mesh.shape["tp"]
    peers = KEY_VALUE_HEADS // tp
    planes = seq // peers
    grouped = (
        tp == 1
        and seq % peers == 0
        and planes >= 3
        and 2 * peers * STRETCH == WINDOW_LENGTH
    )

    def call(*args):
        tokens = args[0].shape[0] // seq
        if grouped and tokens == STRETCH:
            devices = mesh.devices.reshape(planes, peers, tp)
            inner = Mesh(devices, ("plane", "peer", "tp"))
            line, body = ("plane", "peer"), functools.partial(head_sharded, planes)
        else:
            inner, line, body = mesh, "seq", on_device
        split = P(line, "tp")
        return jax.shard_map(
            body,
            mesh=inner,
            in_specs=(split, split, split, P("tp"), split, split, P("tp"), P("tp", None)),
            out_specs=(split, split),
            check_vma=False,
        )(*args)

    return call
```

```python
import functools
import math

import jax
import jax.numpy as jnp
from jax import lax
from jax.experimental import pallas as pl
from jax.experimental.pallas import tpu as pltpu
from jax.sharding import Mesh
from jax.sharding import PartitionSpec as P

QUERY_HEADS = 32
KEY_VALUE_HEADS = 8
HEAD_SIZE = 128
SH = 64
SP = 64
NS = 128
WINDOW_LENGTH = 2048
STRETCH = 128


EPSILON = 1e-05


def shifted(block, axis, distance):
    devices = range(lax.axis_size(axis))
    route = [(i - distance, i) for i in devices if i - distance in devices]
    return lax.ppermute(block, axis, route)


def prefix(x, axis, combine, identity):
    peers, index = (lax.axis_size(axis), lax.axis_index(axis))
    everything = jax.tree.map(lambda part: lax.all_gather(part, axis), x)
    start = jax.tree.map(
        lambda part, zero: jnp.broadcast_to(jnp.asarray(zero, part.dtype), part.shape), x, identity
    )

    def step(k, before):
        reached = k < index
        new = combine(before, jax.tree.map(lambda part: part[k], everything))
        return jax.tree.map(lambda a, b: jnp.where(reached, a, b), new, before)

    return lax.fori_loop(0, peers, step, start)


def combine_states(earlier, later):
    return (earlier[0] * later[0], later[0][..., None, None] * earlier[1] + later[1])


def attention(queries, rotated_keys, values):
    tok_rows = queries.shape[0]
    seq_index = lax.axis_index("seq")
    reach = WINDOW_LENGTH // tok_rows
    kv_local = rotated_keys.shape[1] // HEAD_SIZE
    group_length = QUERY_HEADS // KEY_VALUE_HEADS
    paired = jnp.stack([rotated_keys, values], 0)
    moving = paired
    arrived = []
    for counter in range(reach):
        moving = shifted(moving, "seq", 1)
        arrived.append(moving)
    kv_blocks = arrived[::-1]
    window_kv = jnp.concatenate(kv_blocks + [paired], 1)
    grouped = queries.reshape(tok_rows, kv_local, group_length, HEAD_SIZE)
    score_scale = 1.0 / math.sqrt(HEAD_SIZE)
    query_pos = seq_index * tok_rows + jnp.arange(tok_rows, dtype=jnp.int32)
    base_pos = (seq_index - reach) * tok_rows

    def block_scores(key_block):
        key_row_block = lax.dynamic_slice_in_dim(
            window_kv[0], key_block * tok_rows, tok_rows, 0
        ).reshape(tok_rows, kv_local, HEAD_SIZE)
        scores = (
            jnp.einsum("tkgd,skd->kgts", grouped, key_row_block, preferred_element_type=jnp.float32)
            * score_scale
        )
        key_pos = base_pos + key_block * tok_rows + jnp.arange(tok_rows, dtype=jnp.int32)
        allowed = (
            (key_pos[None, :] <= query_pos[:, None])
            & (key_pos[None, :] > query_pos[:, None] - WINDOW_LENGTH)
            & (key_pos[None, :] >= 0)
        )
        return jnp.where(allowed[None, None], scores, -jnp.inf)

    def visit_order(counter):
        return (counter + reach) % (reach + 1)

    def totals(counter, running):
        row_max, row_sum = running
        scores = block_scores(visit_order(counter))
        new_max = jnp.maximum(row_max, jnp.max(scores, axis=3))
        rescale = jnp.exp(row_max - new_max)
        row_sum = row_sum * rescale + jnp.sum(jnp.exp(scores - new_max[..., None]), axis=3)
        return (new_max, row_sum)

    max_init = jnp.full((kv_local, group_length, tok_rows), -jnp.inf, jnp.float32)
    row_max, row_sum = lax.fori_loop(0, reach + 1, totals, (max_init, jnp.zeros_like(max_init)))

    def weighted(counter, accumulated):
        key_block = visit_order(counter)
        scores = block_scores(key_block)
        value_row_block = lax.dynamic_slice_in_dim(
            window_kv[1], key_block * tok_rows, tok_rows, 0
        ).reshape(tok_rows, kv_local, HEAD_SIZE)
        probs = (jnp.exp(scores - row_max[..., None]) / row_sum[..., None]).astype(jnp.bfloat16)
        return accumulated + jnp.einsum(
            "kgts,skd->kgtd", probs, value_row_block, preferred_element_type=jnp.float32
        )

    acc_init = jnp.zeros((kv_local, group_length, tok_rows, HEAD_SIZE), jnp.float32)
    accumulated = lax.fori_loop(0, reach + 1, weighted, acc_init)
    mixed_rows = jnp.transpose(accumulated, (2, 0, 1, 3))
    return mixed_rows.astype(jnp.bfloat16).reshape(tok_rows, kv_local * group_length * HEAD_SIZE)


def core(inputs, decay_rates, decay_codes, gate_input, norm_gain, bc_weight):
    tok_rows = inputs.shape[0]
    head_count = decay_rates.shape[0]
    channels = SH * SP
    as_float = inputs.astype(jnp.float32)
    own_squares = jnp.sum(as_float * as_float, axis=1)
    partial_value = jnp.dot(inputs, bc_weight, preferred_element_type=jnp.float32)
    total_squares = lax.psum(own_squares, "tp")
    spread = jnp.sqrt(total_squares / channels + EPSILON)[:, None]
    projected = lax.psum(partial_value / spread, "tp")
    normed = (as_float / spread).astype(jnp.bfloat16)
    projected = projected.astype(jnp.bfloat16)
    stretch_count = tok_rows // STRETCH
    x_stretches = normed.reshape(stretch_count, STRETCH, head_count, SP)
    b_stretches = projected[:, :NS].reshape(stretch_count, STRETCH, NS)
    c_stretches = projected[:, NS:].reshape(stretch_count, STRETCH, NS)
    summed_codes = jnp.cumsum(
        decay_codes.reshape(stretch_count, STRETCH, head_count), axis=1, dtype=jnp.int32
    )
    log_decay = -decay_rates * summed_codes.astype(jnp.float32)
    decay_by_head = jnp.transpose(log_decay, (0, 2, 1))
    gram_matrix = jnp.einsum(
        "ctn,csn->cts", c_stretches, b_stretches, preferred_element_type=jnp.float32
    )
    lower_mask = jnp.arange(STRETCH)[:, None] >= jnp.arange(STRETCH)[None, :]
    decay_gaps = jnp.where(
        lower_mask, decay_by_head[..., :, None] - decay_by_head[..., None, :], 0.0
    )
    mixing = jnp.where(lower_mask, gram_matrix[:, None] * jnp.exp(decay_gaps), 0.0).astype(
        jnp.bfloat16
    )
    y_local = jnp.einsum("chts,cshp->cthp", mixing, x_stretches, preferred_element_type=jnp.float32)
    tail_decay = jnp.exp(decay_by_head[..., -1:] - decay_by_head)
    b_weighted = (b_stretches.astype(jnp.float32)[:, None] * tail_decay[..., None]).astype(
        jnp.bfloat16
    )
    contrib = jnp.einsum(
        "chsn,cshp->chnp", b_weighted, x_stretches, preferred_element_type=jnp.float32
    )
    stretch_decay = jnp.exp(decay_by_head[..., -1])
    carried_decay = jnp.ones((head_count,), jnp.float32)
    carried_state = jnp.zeros((head_count, NS, SP), jnp.float32)
    carried_state = stretch_decay[0][:, None, None] * carried_state + contrib[0]
    carried_decay = carried_decay * stretch_decay[0]
    unused_decay, entering = prefix(
        (carried_decay, carried_state),
        "seq",
        combine_states,
        (jnp.ones_like(carried_decay), jnp.zeros_like(carried_state)),
    )
    states = [entering]
    stacked = jnp.stack(states, 0)
    c_weighted = c_stretches.astype(jnp.float32)[:, None] * jnp.exp(decay_by_head)[..., None]
    y_carried = jnp.einsum(
        "chtn,chnp->cthp",
        c_weighted,
        stacked,
        precision=lax.Precision.HIGHEST,
        preferred_element_type=jnp.float32,
    )
    outputs = (y_local + y_carried).reshape(tok_rows, head_count * SP)
    gated_out = outputs * jax.nn.silu(gate_input.astype(jnp.float32))
    gate_squares = lax.psum(jnp.sum(gated_out * gated_out, axis=1), "tp")
    out_scale = jnp.sqrt(gate_squares / channels + EPSILON)[:, None]
    return gated_out / out_scale * norm_gain


def on_device(
    queries, rotated_keys, values, decay_rates, decay_codes, gate_input, norm_gain, bc_weight
):
    attended = attention(queries, rotated_keys, values)
    first_pass = core(attended, decay_rates, decay_codes, gate_input, norm_gain, bc_weight)
    pass_input = first_pass.astype(jnp.bfloat16)
    second_pass = core(pass_input, decay_rates, decay_codes, gate_input, norm_gain, bc_weight)
    return (first_pass, second_pass)


F32 = jnp.float32
BF16 = jnp.bfloat16
LANES = 128
INNER = (((1,), (1,)), ((), ()))
VMEM_BYTES = 24 * 1024 * 1024


def dot(a, b, dims=(((1,), (0,)), ((), ()))):
    return lax.dot_general(a, b, dims, preferred_element_type=F32)


def lane_select(low, high):
    lane = lax.broadcasted_iota(jnp.int32, (1, LANES), 1)
    return jnp.where(lane < SP, low, high)


def split_rows(*rows):
    which = lax.broadcasted_iota(jnp.int32, (16, LANES), 0)
    tile = jnp.zeros((16, LANES), F32)
    for i, row in enumerate(rows):
        for n in range(3):
            piece = row.astype(BF16).astype(F32)
            tile = jnp.where(which == 3 * i + n, piece, tile)
            row = row - piece
    return jnp.concatenate([tile, jnp.zeros_like(tile)], 1).astype(BF16)


def joined_row(pieces, i):
    return pieces[3 * i : 3 * i + 1] + pieces[3 * i + 1 : 3 * i + 2] + pieces[3 * i + 2 : 3 * i + 3]


def column(row):
    return jnp.broadcast_to(row, (LANES, LANES)).T


def pack_kv_kernel(k_ref, v_ref, out_ref):
    for p in range(out_ref.shape[0]):
        cols = pl.ds(p * LANES, LANES)
        out_ref[p, :LANES, :] = k_ref[:, cols]
        out_ref[p, LANES:, :] = v_ref[:, cols]


def pack_heads_kernel(x_ref, *rest):
    out_ref = rest[-1]
    peers = out_ref.shape[0]
    heads = x_ref.shape[1] // LANES // peers
    for p in range(peers):
        for h in range(heads):
            cols = pl.ds((p * heads + h) * LANES, LANES)
            out_ref[p, pl.ds(h * LANES, LANES), :] = x_ref[:, cols]
        if len(rest) == 2:
            out_ref[p, pl.ds(heads * LANES, 16), :] = rest[0][p]


def attend_kernel(
    place_ref, q_ref, ko_ref, vo_ref, k1_ref, v1_ref, k2_ref, v2_ref, bc_ref, x_ref, part_ref, s_ref
):
    j = pl.program_id(0)
    plane = place_ref[0]
    blocks = ko_ref.shape[0]
    rows = q_ref.shape[1]
    q = q_ref[0]
    bias1 = jnp.where(plane >= 1, 0.0, -jnp.inf).astype(F32)
    bias2 = jnp.where(plane >= 2, 0.0, -jnp.inf).astype(F32)
    lane = lax.broadcasted_iota(jnp.int32, (1, 2 * LANES), 1)
    t_pos = lax.broadcasted_iota(jnp.int32, (rows, LANES), 0) % LANES
    s_pos = lax.broadcasted_iota(jnp.int32, (rows, LANES), 1)
    causal = s_pos <= t_pos
    half = blocks // 2

    def mixed(i, own_ref, far_ref):
        return jnp.where(i < j, own_ref[i], far_ref[i + 1])

    top = None
    for i in range(2 * half):
        if i < half:
            keys = k1_ref[2 * i : 2 * i + 2].reshape(2 * LANES, HEAD_SIZE)
            s = dot(q, keys, INNER) + bias1
        else:
            a = 2 * (i - half)
            first = mixed(a, ko_ref, k2_ref)
            bias_a = jnp.where(a < j, 0.0, bias2)
            if i < 2 * half - 1:
                keys = jnp.concatenate([first, mixed(a + 1, ko_ref, k2_ref)], 0)
                bias_b = jnp.where(a + 1 < j, 0.0, bias2)
                s = dot(q, keys, INNER) + jnp.where(lane < LANES, bias_a, bias_b)
            else:
                keys = jnp.concatenate([first, ko_ref[j]], 0)
                s = dot(q, keys, INNER)
                edge = dot(q, k2_ref[j], INNER) + bias2
                s = jnp.concatenate(
                    [s[:, :LANES] + bias_a, jnp.where(causal, s[:, LANES:], edge)], 1
                )
        s_ref[i] = s
        high = jnp.maximum(s[:, :LANES], s[:, LANES:])
        top = high if top is None else jnp.maximum(top, high)
    factor = math.log2(math.e) / math.sqrt(HEAD_SIZE)
    top = jnp.max(top, axis=1, keepdims=True) * factor
    weight = jnp.zeros((rows, LANES), F32)
    for i in range(2 * half):
        p = jnp.exp2(s_ref[i] * factor - top)
        s_ref[i] = p
        weight += p[:, :LANES] + p[:, LANES:]
    weight = 1.0 / jnp.sum(weight, axis=1, keepdims=True)
    total = jnp.zeros((rows, HEAD_SIZE), F32)
    for i in range(2 * half):
        p = (s_ref[i] * weight).astype(BF16)
        if i < half:
            vals = v1_ref[2 * i : 2 * i + 2].reshape(2 * LANES, HEAD_SIZE)
        else:
            a = 2 * (i - half)
            first = mixed(a, vo_ref, v2_ref)
            if i < 2 * half - 1:
                vals = jnp.concatenate([first, mixed(a + 1, vo_ref, v2_ref)], 0)
            else:
                last = p[:, LANES:]
                zero = jnp.zeros_like(last)
                far = jnp.where(causal, zero, last)
                p = jnp.concatenate([p[:, :LANES], jnp.where(causal, last, zero)], 1)
                vals = jnp.concatenate([first, vo_ref[j]], 0)
                total += dot(far, v2_ref[j])
        total += dot(p, vals)
    x = total.astype(BF16)
    x_ref[0] = x
    heads = rows // LANES
    part = jnp.zeros((LANES, 2 * NS), F32)
    squares = jnp.zeros((LANES, LANES), F32)
    for h in range(heads):
        piece = x[h * LANES : (h + 1) * LANES]
        part += dot(piece, bc_ref[pl.ds(h * LANES, LANES), :])
        wide = piece.astype(F32)
        squares += wide * wide
    high = squares.astype(BF16)
    low = (squares - high.astype(F32)).astype(BF16)
    row_ones = jnp.ones((16, LANES), BF16)
    row = dot(row_ones, high, INNER) + dot(row_ones, low, INNER)
    part_ref[0, :LANES, :] = part
    part_ref[0, LANES:, :LANES] = row[:8]
    part_ref[0, LANES:, LANES:] = jnp.zeros_like(row[:8])


def project_kernel(channels, part_ref, out_ref):
    total = part_ref[0]
    for i in range(1, part_ref.shape[0]):
        total += part_ref[i]
    inverse = 1.0 / jnp.sqrt(total[LANES : LANES + 1, :LANES] / channels + EPSILON)
    scale = column(inverse)
    out_ref[:LANES, :NS] = (total[:LANES, :NS] * scale).astype(BF16)
    out_ref[:LANES, NS:] = (total[:LANES, NS:] * scale).astype(BF16)
    out_ref[LANES:, :] = split_rows(inverse)


def code_sums(codes):
    u = lax.broadcasted_iota(jnp.int32, (LANES, LANES), 0)
    t = lax.broadcasted_iota(jnp.int32, (LANES, LANES), 1)
    upper = jnp.where(u <= t, 1.0, 0.0).astype(BF16)
    sums = dot(codes, upper)
    return sums[:8] * 128.0 + sums[8:]


def columns_of(by_row):
    pad = jnp.zeros((LANES - by_row.shape[0], LANES), F32)
    return jnp.concatenate([by_row, pad], 0).T


def states_kernel(with_gain, x_ref, proj_ref, side_ref, rates_ref, *rest):
    if with_gain:
        gain_ref, *rest = rest
    normed_ref, enter_ref, end_ref, state_ref, count_ref = rest
    peers, wide = x_ref.shape[:2]
    pairs = wide // LANES
    rates = rates_ref[...]
    state_ref[...] = jnp.zeros_like(state_ref)
    count_ref[...] = jnp.zeros_like(count_ref)

    @pl.loop(0, peers)
    def _(k):
        sums = code_sums(side_ref[k, pl.ds(wide, 16), :])
        last = sums[:, LANES - 1 :]
        weights = jnp.exp(-rates * (last - sums))
        block_decay = jnp.exp(-rates * last)
        count_ref[...] += jnp.broadcast_to(last, count_ref.shape)
        b_across = proj_ref[k, :LANES, :NS].astype(F32).T
        pieces = proj_ref[k, LANES:, :LANES].astype(F32)
        inverse = column(joined_row(pieces, 0))
        if with_gain:
            out_inverse = column(joined_row(pieces, 1))
        for pair in range(pairs):
            rows = pl.ds(pair * LANES, LANES)
            x = x_ref[k, rows, :].astype(F32)
            if with_gain:
                x = x * out_inverse * gain_ref[pair : pair + 1, :]
                x = x.astype(BF16).astype(F32)
            x = (x * inverse).astype(BF16)
            normed_ref[k, rows, :] = x
            h = 2 * pair
            b = jnp.concatenate(
                [b_across * weights[h : h + 1], b_across * weights[h + 1 : h + 2]], 0
            ).astype(BF16)
            both = dot(b, x)
            contrib = lane_select(both[:NS], both[NS:])
            state = state_ref[rows, :]
            enter_ref[k, rows, :] = state
            decay = lane_select(block_decay[h : h + 1], block_decay[h + 1 : h + 2])
            state_ref[rows, :] = decay * state + contrib

    end_ref[:wide, :] = state_ref[...].astype(BF16)
    whole = jnp.exp(-rates * count_ref[...])
    which = lax.broadcasted_iota(jnp.int32, (16, LANES), 0)
    tile = jnp.zeros((16, LANES), F32)
    for pair in range(pairs):
        row = lane_select(whole[2 * pair : 2 * pair + 1], whole[2 * pair + 1 : 2 * pair + 2])
        for n in range(3):
            piece = row.astype(BF16).astype(F32)
            tile = jnp.where(which == 3 * pair + n, piece, tile)
            row = row - piece
    end_ref[wide:, :] = tile.astype(BF16)


def carried(c_twice, grown, states):
    parts = []
    for state in states:
        high = state.astype(BF16)
        low = (state - high.astype(F32)).astype(BF16)
        parts.append(jnp.concatenate([high, low], 0))
    out = dot(c_twice, jnp.concatenate(parts, 1))
    scaled = []
    for pair in range(len(states)):
        scale = lane_select(grown[:, 2 * pair : 2 * pair + 1], grown[:, 2 * pair + 1 : 2 * pair + 2])
        scaled.append(scale * out[:, pair * LANES : (pair + 1) * LANES])
    return scaled


def local_kernel(x_ref, proj_ref, side_ref, rates_ref, enter_ref, y_ref, silu_ref):
    peers, wide = x_ref.shape[:2]
    pairs = wide // LANES
    t = lax.broadcasted_iota(jnp.int32, (LANES, LANES), 0)
    s = lax.broadcasted_iota(jnp.int32, (LANES, LANES), 1)
    lower = t >= s

    @pl.loop(0, peers)
    def _(k):
        ell = -rates_ref[...] * code_sums(side_ref[k, pl.ds(wide, 16), :])
        ell_col = columns_of(ell)
        b = proj_ref[k, :LANES, :NS]
        c = proj_ref[k, :LANES, NS:]
        gram = dot(c, b, INNER)
        states = [enter_ref[k, pl.ds(pair * NS, NS), :] for pair in range(pairs)]
        carry = carried(jnp.concatenate([c, c], 1), jnp.exp(ell_col), states)
        for pair in range(pairs):
            rows = pl.ds(pair * LANES, LANES)
            mixes = []
            for h in (2 * pair, 2 * pair + 1):
                gap = jnp.where(lower, ell_col[:, h : h + 1] - ell[h : h + 1], -jnp.inf)
                mixes.append((gram * jnp.exp(gap)).astype(BF16))
            x = x_ref[k, rows, :]
            zero = jnp.zeros_like(x)
            right = jnp.concatenate([lane_select(x, zero), lane_select(zero, x)], 0)
            y_ref[k, rows, :] = dot(jnp.concatenate(mixes, 1), right) + carry[pair]
            gate = side_ref[k, rows, :].astype(F32)
            silu_ref[k, rows, :] = gate / (1.0 + jnp.exp(-gate))


def gated_kernel(planes, with_full, y_ref, silu_ref, proj_ref, side_ref, rates_ref, *rest):
    ends, rest = rest[: planes - 1], rest[planes - 1 :]
    out_ref = rest[0]
    count_ref, enter_ref = rest[-2:]
    peers, wide = y_ref.shape[:2]
    pairs = wide // LANES
    rates = rates_ref[...]
    count_ref[...] = jnp.zeros_like(count_ref)
    for pair in range(pairs):
        rows = pl.ds(pair * LANES, LANES)
        state = ends[-1][rows, :].astype(F32)
        for i in range(planes - 3, -1, -1):
            decay = joined_row(ends[i][wide:, :].astype(F32), pair)
            state = ends[i][rows, :].astype(F32) + decay * state
        enter_ref[rows, :] = state

    @pl.loop(0, peers)
    def _(k):
        sums = code_sums(side_ref[k, pl.ds(wide, 16), :])
        grown = columns_of(jnp.exp(-rates * (sums + count_ref[...])))
        count_ref[...] += jnp.broadcast_to(sums[:, LANES - 1 :], count_ref.shape)
        c = proj_ref[k, :LANES, NS:]
        states = [enter_ref[pl.ds(pair * NS, NS), :] for pair in range(pairs)]
        carry = carried(jnp.concatenate([c, c], 1), grown, states)
        for pair in range(pairs):
            rows = pl.ds(pair * LANES, LANES)
            y = (y_ref[k, rows, :] + carry[pair]) * silu_ref[k, rows, :]
            out_ref[k, rows, :] = y.astype(BF16)
            if with_full:
                rest[1][k, rows, :] = y


def finish_kernel(channels, with_proj, g_ref, gain_ref, *rest):
    if with_proj:
        bc_ref, out_ref, proj_ref = rest
    else:
        (out_ref,) = rest
    parts, wide = g_ref.shape[0], g_ref.shape[1] // LANES
    squares = jnp.zeros((LANES, LANES), F32)
    for p in range(parts):
        for i in range(wide):
            g = g_ref[p, i * LANES : (i + 1) * LANES, :].astype(F32)
            squares += g * g
    inverse = 1.0 / jnp.sqrt(jnp.sum(squares, 1, keepdims=True) / channels + EPSILON)
    scaled = jnp.zeros((LANES, LANES), F32)
    proj = jnp.zeros((LANES, 2 * NS), F32)
    for p in range(parts):
        for i in range(wide):
            n = p * wide + i
            g = g_ref[p, i * LANES : (i + 1) * LANES, :].astype(F32)
            out = g * inverse * gain_ref[n : n + 1, :]
            out_ref[:, n * LANES : (n + 1) * LANES] = out
            if with_proj:
                x = out.astype(BF16)
                proj += dot(x, bc_ref[n * LANES : (n + 1) * LANES, :])
                x = x.astype(F32)
                scaled += x * x
    if with_proj:
        mean = jnp.sum(scaled, 1, keepdims=True) / channels
        both = 1.0 / jnp.sqrt(mean + EPSILON)
        proj_ref[:LANES, :] = (proj * both).astype(BF16)
        wide = jnp.broadcast_to(both, (LANES, LANES)).T
        proj_ref[LANES:, :] = split_rows(wide[:1], jnp.broadcast_to(inverse, wide.shape).T[:1])


def params(**kw):
    return pltpu.CompilerParams(vmem_limit_bytes=VMEM_BYTES, **kw)


def cost(flops, nbytes, exps=0):
    return pl.CostEstimate(flops=flops, bytes_accessed=nbytes, transcendentals=exps)


def whole_block(shape):
    return pl.BlockSpec(shape, lambda *_: (0,) * len(shape))


def head_sharded(
    planes, queries, rotated_keys, values, decay_rates, decay_codes, gate_input, norm_gain, bc_weight
):
    tokens, channels = queries.shape
    peers = lax.axis_size("peer")
    wide = channels // peers
    pairs = wide // LANES
    heads = decay_codes.shape[1] // peers
    peer = lax.axis_index("peer")
    place = jnp.stack([lax.axis_index("plane"), peer]).astype(jnp.int32)

    def moved(x, distance):
        return lax.ppermute(x, "plane", [(i, i + distance) for i in range(planes - distance)])

    kv = pl.pallas_call(
        pack_kv_kernel,
        out_shape=jax.ShapeDtypeStruct((peers, 2 * tokens, HEAD_SIZE), BF16),
        compiler_params=params(),
        name="pack_kv",
    )(rotated_keys, values)
    kv_own = lax.all_to_all(kv, "peer", 0, 0)
    kv_one = moved(kv_own, 1)
    kv_two = moved(kv_one, 1)

    packed = pl.pallas_call(
        pack_heads_kernel,
        out_shape=jax.ShapeDtypeStruct((peers, wide, LANES), BF16),
        compiler_params=params(),
        name="pack_queries",
    )(queries)
    arrived = lax.all_to_all(packed, "peer", 0, 0)

    coded = jnp.stack([decay_codes >> 7, decay_codes & 127], 0).astype(BF16)
    coded = jnp.transpose(coded.reshape(2, tokens, peers, heads), (2, 0, 3, 1))
    coded = coded.reshape(peers, 2 * heads, tokens)
    packed = pl.pallas_call(
        pack_heads_kernel,
        out_shape=jax.ShapeDtypeStruct((peers, wide + 16, LANES), BF16),
        compiler_params=params(),
        name="pack_gates",
    )(gate_input, coded)
    side = lax.all_to_all(packed, "peer", 0, 0)

    def keys_spec(which):
        return pl.BlockSpec((peers, tokens, HEAD_SIZE), lambda j, s: (0, which, 0))

    def block(rows, which=0, lanes=LANES):
        return pl.BlockSpec((1, rows, lanes), lambda j, s: (j, which, 0))

    proj_rows = tokens + 16
    attended, partial = pl.pallas_call(
        attend_kernel,
        grid_spec=pltpu.PrefetchScalarGridSpec(
            num_scalar_prefetch=1,
            grid=(peers,),
            in_specs=[block(wide)]
            + [keys_spec(0), keys_spec(1)] * 3
            + [pl.BlockSpec((wide, 2 * NS), lambda j, s: (s[1], 0))],
            out_specs=[block(wide), block(tokens + 8, 0, 2 * NS)],
            scratch_shapes=[pltpu.VMEM((peers, wide, 2 * tokens), F32)],
        ),
        out_shape=[
            jax.ShapeDtypeStruct((peers, wide, LANES), BF16),
            jax.ShapeDtypeStruct((peers, tokens + 8, 2 * NS), F32),
        ],
        compiler_params=params(),
        cost_estimate=cost(5 * 10**9, 4 * 10**6, 9 * 10**6),
        name="attend",
    )(place, arrived, kv_own, kv_own, kv_one, kv_one, kv_two, kv_two, bc_weight)

    shares = lax.all_to_all(partial, "peer", 0, 0)
    proj = pl.pallas_call(
        functools.partial(project_kernel, channels),
        in_specs=[whole_block((peers, tokens + 8, 2 * NS))],
        out_specs=whole_block((proj_rows, 2 * NS)),
        out_shape=jax.ShapeDtypeStruct((proj_rows, 2 * NS), BF16),
        name="project",
    )(shares)

    rates = lax.dynamic_slice_in_dim(decay_rates, peer * heads, heads, 0)
    rates = jnp.broadcast_to(rates[:, None], (heads, LANES))
    gains = lax.dynamic_slice_in_dim(norm_gain.reshape(peers, pairs, LANES), peer, 1, 0)[0]
    full_shape = jax.ShapeDtypeStruct((peers, wide, LANES), F32)
    half_shape = jax.ShapeDtypeStruct((peers, wide, LANES), BF16)

    def ssd(x, projected, with_gain):
        operands = [x, projected, side, rates] + ([gains] if with_gain else [])
        normed, entering, end = pl.pallas_call(
            functools.partial(states_kernel, with_gain),
            out_shape=[half_shape, full_shape, jax.ShapeDtypeStruct((wide + 16, LANES), BF16)],
            scratch_shapes=[pltpu.VMEM((wide, LANES), F32), pltpu.VMEM((heads, LANES), F32)],
            compiler_params=params(),
            cost_estimate=cost(10**9, 4 * 10**6),
            name="states",
        )(*operands)
        earlier = [moved(end, i) for i in range(1, planes)]
        y, silu = pl.pallas_call(
            local_kernel,
            out_shape=[full_shape, full_shape],
            compiler_params=params(),
            cost_estimate=cost(2 * 10**9, 5 * 10**6, 10**6),
            name="local",
        )(normed, projected, side, rates, entering)
        return pl.pallas_call(
            functools.partial(gated_kernel, planes, not with_gain),
            out_shape=[half_shape] if with_gain else [half_shape, full_shape],
            scratch_shapes=[pltpu.VMEM((heads, LANES), F32), pltpu.VMEM((wide, LANES), F32)],
            compiler_params=params(),
            cost_estimate=cost(10**9, 5 * 10**6, 10**6),
            name="gated",
        )(y, silu, projected, side, rates, *earlier)

    gain_rows = norm_gain.reshape(channels // LANES, LANES)
    gathered = (peers, wide, LANES)

    projected = lax.all_gather(proj, "peer")
    gated, full = ssd(attended, projected, False)
    first, proj = pl.pallas_call(
        functools.partial(finish_kernel, channels, True),
        in_specs=[
            whole_block(gathered),
            whole_block(gain_rows.shape),
            whole_block((channels, 2 * NS)),
        ],
        out_specs=[whole_block((tokens, channels)), whole_block((proj_rows, 2 * NS))],
        out_shape=[
            jax.ShapeDtypeStruct((tokens, channels), F32),
            jax.ShapeDtypeStruct((proj_rows, 2 * NS), BF16),
        ],
        compiler_params=params(),
        name="finish_first",
    )(lax.all_to_all(gated, "peer", 0, 0), gain_rows, bc_weight)
    projected = lax.all_gather(proj, "peer")
    (gated,) = ssd(full, projected, True)
    second = pl.pallas_call(
        functools.partial(finish_kernel, channels, False),
        in_specs=[whole_block(gathered), whole_block(gain_rows.shape)],
        out_specs=whole_block((tokens, channels)),
        out_shape=jax.ShapeDtypeStruct((tokens, channels), F32),
        compiler_params=params(),
        name="finish_second",
    )(lax.all_to_all(gated, "peer", 0, 0), gain_rows)
    return first, second


def solution(mesh):
    seq, tp = mesh.shape["seq"], mesh.shape["tp"]
    peers = KEY_VALUE_HEADS // tp
    planes = seq // peers
    grouped = (
        tp == 1
        and seq % peers == 0
        and planes >= 3
        and 2 * peers * STRETCH == WINDOW_LENGTH
    )

    def call(*args):
        tokens = args[0].shape[0] // seq
        if grouped and tokens == STRETCH:
            devices = mesh.devices.reshape(planes, peers, tp)
            inner = Mesh(devices, ("plane", "peer", "tp"))
            line, body = ("plane", "peer"), functools.partial(head_sharded, planes)
        else:
            inner, line, body = mesh, "seq", on_device
        split = P(line, "tp")
        return jax.shard_map(
            body,
            mesh=inner,
            in_specs=(split, split, split, P("tp"), split, split, P("tp"), P("tp", None)),
            out_specs=(split, split),
            check_vma=False,
        )(*args)

    return call
```

```python
import functools
import math

import jax
import jax.numpy as jnp
from jax import lax
from jax.experimental import pallas as pl
from jax.experimental.pallas import tpu as pltpu
from jax.sharding import Mesh
from jax.sharding import PartitionSpec as P

QUERY_HEADS = 32
KEY_VALUE_HEADS = 8
HEAD_SIZE = 128
SH = 64
SP = 64
NS = 128
WINDOW_LENGTH = 2048
STRETCH = 128


EPSILON = 1e-05


def shifted(block, axis, distance):
    devices = range(lax.axis_size(axis))
    route = [(i - distance, i) for i in devices if i - distance in devices]
    return lax.ppermute(block, axis, route)


def prefix(x, axis, combine, identity):
    peers, index = (lax.axis_size(axis), lax.axis_index(axis))
    everything = jax.tree.map(lambda part: lax.all_gather(part, axis), x)
    start = jax.tree.map(
        lambda part, zero: jnp.broadcast_to(jnp.asarray(zero, part.dtype), part.shape), x, identity
    )

    def step(k, before):
        reached = k < index
        new = combine(before, jax.tree.map(lambda part: part[k], everything))
        return jax.tree.map(lambda a, b: jnp.where(reached, a, b), new, before)

    return lax.fori_loop(0, peers, step, start)


def combine_states(earlier, later):
    return (earlier[0] * later[0], later[0][..., None, None] * earlier[1] + later[1])


def attention(queries, rotated_keys, values):
    tok_rows = queries.shape[0]
    seq_index = lax.axis_index("seq")
    reach = WINDOW_LENGTH // tok_rows
    kv_local = rotated_keys.shape[1] // HEAD_SIZE
    group_length = QUERY_HEADS // KEY_VALUE_HEADS
    paired = jnp.stack([rotated_keys, values], 0)
    moving = paired
    arrived = []
    for counter in range(reach):
        moving = shifted(moving, "seq", 1)
        arrived.append(moving)
    kv_blocks = arrived[::-1]
    window_kv = jnp.concatenate(kv_blocks + [paired], 1)
    grouped = queries.reshape(tok_rows, kv_local, group_length, HEAD_SIZE)
    score_scale = 1.0 / math.sqrt(HEAD_SIZE)
    query_pos = seq_index * tok_rows + jnp.arange(tok_rows, dtype=jnp.int32)
    base_pos = (seq_index - reach) * tok_rows

    def block_scores(key_block):
        key_row_block = lax.dynamic_slice_in_dim(
            window_kv[0], key_block * tok_rows, tok_rows, 0
        ).reshape(tok_rows, kv_local, HEAD_SIZE)
        scores = (
            jnp.einsum("tkgd,skd->kgts", grouped, key_row_block, preferred_element_type=jnp.float32)
            * score_scale
        )
        key_pos = base_pos + key_block * tok_rows + jnp.arange(tok_rows, dtype=jnp.int32)
        allowed = (
            (key_pos[None, :] <= query_pos[:, None])
            & (key_pos[None, :] > query_pos[:, None] - WINDOW_LENGTH)
            & (key_pos[None, :] >= 0)
        )
        return jnp.where(allowed[None, None], scores, -jnp.inf)

    def visit_order(counter):
        return (counter + reach) % (reach + 1)

    def totals(counter, running):
        row_max, row_sum = running
        scores = block_scores(visit_order(counter))
        new_max = jnp.maximum(row_max, jnp.max(scores, axis=3))
        rescale = jnp.exp(row_max - new_max)
        row_sum = row_sum * rescale + jnp.sum(jnp.exp(scores - new_max[..., None]), axis=3)
        return (new_max, row_sum)

    max_init = jnp.full((kv_local, group_length, tok_rows), -jnp.inf, jnp.float32)
    row_max, row_sum = lax.fori_loop(0, reach + 1, totals, (max_init, jnp.zeros_like(max_init)))

    def weighted(counter, accumulated):
        key_block = visit_order(counter)
        scores = block_scores(key_block)
        value_row_block = lax.dynamic_slice_in_dim(
            window_kv[1], key_block * tok_rows, tok_rows, 0
        ).reshape(tok_rows, kv_local, HEAD_SIZE)
        probs = (jnp.exp(scores - row_max[..., None]) / row_sum[..., None]).astype(jnp.bfloat16)
        return accumulated + jnp.einsum(
            "kgts,skd->kgtd", probs, value_row_block, preferred_element_type=jnp.float32
        )

    acc_init = jnp.zeros((kv_local, group_length, tok_rows, HEAD_SIZE), jnp.float32)
    accumulated = lax.fori_loop(0, reach + 1, weighted, acc_init)
    mixed_rows = jnp.transpose(accumulated, (2, 0, 1, 3))
    return mixed_rows.astype(jnp.bfloat16).reshape(tok_rows, kv_local * group_length * HEAD_SIZE)


def core(inputs, decay_rates, decay_codes, gate_input, norm_gain, bc_weight):
    tok_rows = inputs.shape[0]
    head_count = decay_rates.shape[0]
    channels = SH * SP
    as_float = inputs.astype(jnp.float32)
    own_squares = jnp.sum(as_float * as_float, axis=1)
    partial_value = jnp.dot(inputs, bc_weight, preferred_element_type=jnp.float32)
    total_squares = lax.psum(own_squares, "tp")
    spread = jnp.sqrt(total_squares / channels + EPSILON)[:, None]
    projected = lax.psum(partial_value / spread, "tp")
    normed = (as_float / spread).astype(jnp.bfloat16)
    projected = projected.astype(jnp.bfloat16)
    stretch_count = tok_rows // STRETCH
    x_stretches = normed.reshape(stretch_count, STRETCH, head_count, SP)
    b_stretches = projected[:, :NS].reshape(stretch_count, STRETCH, NS)
    c_stretches = projected[:, NS:].reshape(stretch_count, STRETCH, NS)
    summed_codes = jnp.cumsum(
        decay_codes.reshape(stretch_count, STRETCH, head_count), axis=1, dtype=jnp.int32
    )
    log_decay = -decay_rates * summed_codes.astype(jnp.float32)
    decay_by_head = jnp.transpose(log_decay, (0, 2, 1))
    gram_matrix = jnp.einsum(
        "ctn,csn->cts", c_stretches, b_stretches, preferred_element_type=jnp.float32
    )
    lower_mask = jnp.arange(STRETCH)[:, None] >= jnp.arange(STRETCH)[None, :]
    decay_gaps = jnp.where(
        lower_mask, decay_by_head[..., :, None] - decay_by_head[..., None, :], 0.0
    )
    mixing = jnp.where(lower_mask, gram_matrix[:, None] * jnp.exp(decay_gaps), 0.0).astype(
        jnp.bfloat16
    )
    y_local = jnp.einsum("chts,cshp->cthp", mixing, x_stretches, preferred_element_type=jnp.float32)
    tail_decay = jnp.exp(decay_by_head[..., -1:] - decay_by_head)
    b_weighted = (b_stretches.astype(jnp.float32)[:, None] * tail_decay[..., None]).astype(
        jnp.bfloat16
    )
    contrib = jnp.einsum(
        "chsn,cshp->chnp", b_weighted, x_stretches, preferred_element_type=jnp.float32
    )
    stretch_decay = jnp.exp(decay_by_head[..., -1])
    carried_decay = jnp.ones((head_count,), jnp.float32)
    carried_state = jnp.zeros((head_count, NS, SP), jnp.float32)
    carried_state = stretch_decay[0][:, None, None] * carried_state + contrib[0]
    carried_decay = carried_decay * stretch_decay[0]
    unused_decay, entering = prefix(
        (carried_decay, carried_state),
        "seq",
        combine_states,
        (jnp.ones_like(carried_decay), jnp.zeros_like(carried_state)),
    )
    states = [entering]
    stacked = jnp.stack(states, 0)
    c_weighted = c_stretches.astype(jnp.float32)[:, None] * jnp.exp(decay_by_head)[..., None]
    y_carried = jnp.einsum(
        "chtn,chnp->cthp",
        c_weighted,
        stacked,
        precision=lax.Precision.HIGHEST,
        preferred_element_type=jnp.float32,
    )
    outputs = (y_local + y_carried).reshape(tok_rows, head_count * SP)
    gated_out = outputs * jax.nn.silu(gate_input.astype(jnp.float32))
    gate_squares = lax.psum(jnp.sum(gated_out * gated_out, axis=1), "tp")
    out_scale = jnp.sqrt(gate_squares / channels + EPSILON)[:, None]
    return gated_out / out_scale * norm_gain


def on_device(
    queries, rotated_keys, values, decay_rates, decay_codes, gate_input, norm_gain, bc_weight
):
    attended = attention(queries, rotated_keys, values)
    first_pass = core(attended, decay_rates, decay_codes, gate_input, norm_gain, bc_weight)
    pass_input = first_pass.astype(jnp.bfloat16)
    second_pass = core(pass_input, decay_rates, decay_codes, gate_input, norm_gain, bc_weight)
    return (first_pass, second_pass)


F32 = jnp.float32
BF16 = jnp.bfloat16
LANES = 128
INNER = (((1,), (1,)), ((), ()))
MIB = 1024 * 1024


def dot(a, b, dims=(((1,), (0,)), ((), ()))):
    return lax.dot_general(a, b, dims, preferred_element_type=F32)


def lane_select(low, high):
    lane = lax.broadcasted_iota(jnp.int32, (1, LANES), 1)
    return jnp.where(lane < SP, low, high)


def split_rows(*rows):
    which = lax.broadcasted_iota(jnp.int32, (16, LANES), 0)
    tile = jnp.zeros((16, LANES), F32)
    for i, row in enumerate(rows):
        for n in range(3):
            piece = row.astype(BF16).astype(F32)
            tile = jnp.where(which == 3 * i + n, piece, tile)
            row = row - piece
    return jnp.concatenate([tile, jnp.zeros_like(tile)], 1).astype(BF16)


def joined_row(pieces, i):
    return pieces[3 * i : 3 * i + 1] + pieces[3 * i + 1 : 3 * i + 2] + pieces[3 * i + 2 : 3 * i + 3]


def column(row):
    return jnp.broadcast_to(row, (LANES, LANES)).T


def pack_kv_kernel(k_ref, v_ref, out_ref):
    for p in range(out_ref.shape[0]):
        cols = pl.ds(p * LANES, LANES)
        out_ref[p, :LANES, :] = k_ref[:, cols]
        out_ref[p, LANES:, :] = v_ref[:, cols]


def pack_heads_kernel(x_ref, *rest):
    out_ref = rest[-1]
    peers = out_ref.shape[0]
    heads = x_ref.shape[1] // LANES // peers
    for p in range(peers):
        for h in range(heads):
            cols = pl.ds((p * heads + h) * LANES, LANES)
            out_ref[p, pl.ds(h * LANES, LANES), :] = x_ref[:, cols]
        if len(rest) == 2:
            out_ref[p, pl.ds(heads * LANES, 16), :] = rest[0][p]


def attend_kernel(
    place_ref, q_ref, ko_ref, vo_ref, k1_ref, v1_ref, k2_ref, v2_ref, bc_ref, x_ref, part_ref, *scores
):
    plane = place_ref[0]
    blocks = ko_ref.shape[0]
    steps, rows = q_ref.shape[:2]
    half = blocks // 2
    count = 2 * half
    unit_rows = 2 * LANES
    splits = rows // unit_rows
    factor = math.log2(math.e) / math.sqrt(HEAD_SIZE)
    bias2 = jnp.where(plane >= 2, 0.0, -jnp.inf).astype(F32)
    lane = lax.broadcasted_iota(jnp.int32, (1, 2 * LANES), 1)
    t_pos = lax.broadcasted_iota(jnp.int32, (unit_rows, LANES), 0) % LANES
    s_pos = lax.broadcasted_iota(jnp.int32, (unit_rows, LANES), 1)
    causal = s_pos <= t_pos

    def unit(n):
        here, part = n // splits, n % splits
        j = pl.program_id(0) * steps + here
        s_ref = scores[n % len(scores)]
        span = pl.ds(part * unit_rows, unit_rows)
        held = {}

        def mixed(i, own_ref, far_ref):
            return jnp.where(i < j, own_ref[i], far_ref[i + 1])

        def score(i):
            q = q_ref[here, span, :]
            if i < half:
                s = dot(q, k1_ref[2 * i : 2 * i + 2].reshape(2 * LANES, HEAD_SIZE), INNER)
                key = "near"
            else:
                a = 2 * (i - half)
                first = mixed(a, ko_ref, k2_ref)
                bias_a = jnp.where(a < j, 0.0, bias2)
                if i < count - 1:
                    bias_b = jnp.where(a + 1 < j, 0.0, bias2)
                    s = dot(q, jnp.concatenate([first, mixed(a + 1, ko_ref, k2_ref)], 0), INNER)
                    s = s + jnp.where(lane < LANES, bias_a, bias_b)
                else:
                    s = dot(q, jnp.concatenate([first, ko_ref[j]], 0), INNER)
                    edge = dot(q, k2_ref[j], INNER) + bias2
                    s = jnp.concatenate(
                        [s[:, :LANES] + bias_a, jnp.where(causal, s[:, LANES:], edge)], 1
                    )
                key = "rest"
            s_ref[i] = s
            high = jnp.maximum(s[:, :LANES], s[:, LANES:])
            held[key] = jnp.maximum(held[key], high) if key in held else high
            if i == count - 1:
                near = jnp.where(plane >= 1, held.pop("near"), -jnp.inf)
                top = jnp.max(jnp.maximum(near, held.pop("rest")), axis=1, keepdims=True) * factor
                held["top"] = top
                held["top_near"] = jnp.where(plane >= 1, top, jnp.inf)

        def weigh(i):
            p = jnp.exp2(s_ref[i] * factor - held["top_near" if i < half else "top"])
            s_ref[i] = p
            both = p[:, :LANES] + p[:, LANES:]
            held["sum"] = held["sum"] + both if "sum" in held else both
            if i == count - 1:
                held["inverse"] = 1.0 / jnp.sum(held.pop("sum"), axis=1, keepdims=True)

        def mix(i):
            p = (s_ref[i] * held["inverse"]).astype(BF16)
            if i < half:
                vals = v1_ref[2 * i : 2 * i + 2].reshape(2 * LANES, HEAD_SIZE)
            else:
                a = 2 * (i - half)
                first = mixed(a, vo_ref, v2_ref)
                if i < count - 1:
                    vals = jnp.concatenate([first, mixed(a + 1, vo_ref, v2_ref)], 0)
                else:
                    last = p[:, LANES:]
                    zero = jnp.zeros_like(last)
                    far = jnp.where(causal, zero, last)
                    p = jnp.concatenate([p[:, :LANES], jnp.where(causal, last, zero)], 1)
                    vals = jnp.concatenate([first, vo_ref[j]], 0)
                    held["total"] += dot(far, v2_ref[j])
            new = dot(p, vals)
            held["total"] = held["total"] + new if "total" in held else new
            if i == count - 1:
                x_ref[here, span, :] = held.pop("total").astype(BF16)

        return score, weigh, mix

    units = [unit(n) for n in range(steps * splits)]
    for phase in range(len(units) + 2):
        for i in range(count):
            for stage in (2, 1, 0):
                n = phase - stage
                if 0 <= n < len(units):
                    units[n][stage](i)
    for here in range(steps):
        part = jnp.zeros((LANES, 2 * NS), F32)
        squares = jnp.zeros((LANES, LANES), F32)
        for h in range(rows // LANES):
            piece = x_ref[here, pl.ds(h * LANES, LANES), :]
            part += dot(piece, bc_ref[pl.ds(h * LANES, LANES), :])
            wide = piece.astype(F32)
            squares += wide * wide
        high = squares.astype(BF16)
        low = (squares - high.astype(F32)).astype(BF16)
        row_ones = jnp.ones((16, LANES), BF16)
        row = dot(row_ones, high, INNER) + dot(row_ones, low, INNER)
        part_ref[here, :LANES, :] = part
        part_ref[here, LANES:, :LANES] = row[:8]
        part_ref[here, LANES:, LANES:] = jnp.zeros_like(row[:8])


def project_kernel(channels, part_ref, out_ref):
    total = part_ref[0]
    for i in range(1, part_ref.shape[0]):
        total += part_ref[i]
    inverse = 1.0 / jnp.sqrt(total[LANES : LANES + 1, :LANES] / channels + EPSILON)
    scale = column(inverse)
    out_ref[:LANES, :NS] = (total[:LANES, :NS] * scale).astype(BF16)
    out_ref[:LANES, NS:] = (total[:LANES, NS:] * scale).astype(BF16)
    out_ref[LANES:, :] = split_rows(inverse)


def code_sums(codes):
    u = lax.broadcasted_iota(jnp.int32, (LANES, LANES), 0)
    t = lax.broadcasted_iota(jnp.int32, (LANES, LANES), 1)
    upper = jnp.where(u <= t, 1.0, 0.0).astype(BF16)
    sums = dot(codes, upper)
    return sums[:8] * 128.0 + sums[8:]


def columns_of(by_row):
    pad = jnp.zeros((LANES - by_row.shape[0], LANES), F32)
    return jnp.concatenate([by_row, pad], 0).T


def states_kernel(with_gain, x_ref, proj_ref, side_ref, rates_ref, *rest):
    if with_gain:
        gain_ref, *rest = rest
    normed_ref, enter_ref, end_ref, state_ref, count_ref = rest
    peers, wide = x_ref.shape[:2]
    pairs = wide // LANES
    rates = rates_ref[...]
    state_ref[...] = jnp.zeros_like(state_ref)
    count_ref[...] = jnp.zeros_like(count_ref)

    @pl.loop(0, peers)
    def _(k):
        sums = code_sums(side_ref[k, pl.ds(wide, 16), :])
        last = sums[:, LANES - 1 :]
        weights = jnp.exp(-rates * (last - sums))
        block_decay = jnp.exp(-rates * last)
        count_ref[...] += jnp.broadcast_to(last, count_ref.shape)
        b_across = proj_ref[k, :LANES, :NS].astype(F32).T
        pieces = proj_ref[k, LANES:, :LANES].astype(F32)
        inverse = column(joined_row(pieces, 0))
        if with_gain:
            out_inverse = column(joined_row(pieces, 1))
        for pair in range(pairs):
            rows = pl.ds(pair * LANES, LANES)
            x = x_ref[k, rows, :].astype(F32)
            if with_gain:
                x = x * out_inverse * gain_ref[pair : pair + 1, :]
                x = x.astype(BF16).astype(F32)
            x = (x * inverse).astype(BF16)
            normed_ref[k, rows, :] = x
            h = 2 * pair
            b = jnp.concatenate(
                [b_across * weights[h : h + 1], b_across * weights[h + 1 : h + 2]], 0
            ).astype(BF16)
            both = dot(b, x)
            contrib = lane_select(both[:NS], both[NS:])
            state = state_ref[rows, :]
            enter_ref[k, rows, :] = state
            decay = lane_select(block_decay[h : h + 1], block_decay[h + 1 : h + 2])
            state_ref[rows, :] = decay * state + contrib

    end_ref[:wide, :] = state_ref[...].astype(BF16)
    whole = jnp.exp(-rates * count_ref[...])
    which = lax.broadcasted_iota(jnp.int32, (16, LANES), 0)
    tile = jnp.zeros((16, LANES), F32)
    for pair in range(pairs):
        row = lane_select(whole[2 * pair : 2 * pair + 1], whole[2 * pair + 1 : 2 * pair + 2])
        for n in range(3):
            piece = row.astype(BF16).astype(F32)
            tile = jnp.where(which == 3 * pair + n, piece, tile)
            row = row - piece
    end_ref[wide:, :] = tile.astype(BF16)


def carried(c_twice, grown, states):
    parts = []
    for state in states:
        high = state.astype(BF16)
        low = (state - high.astype(F32)).astype(BF16)
        parts.append(jnp.concatenate([high, low], 0))
    out = dot(c_twice, jnp.concatenate(parts, 1))
    scaled = []
    for pair in range(len(states)):
        scale = lane_select(grown[:, 2 * pair : 2 * pair + 1], grown[:, 2 * pair + 1 : 2 * pair + 2])
        scaled.append(scale * out[:, pair * LANES : (pair + 1) * LANES])
    return scaled


def local_kernel(x_ref, proj_ref, side_ref, rates_ref, enter_ref, y_ref, silu_ref):
    peers, wide = x_ref.shape[:2]
    pairs = wide // LANES
    t = lax.broadcasted_iota(jnp.int32, (LANES, LANES), 0)
    s = lax.broadcasted_iota(jnp.int32, (LANES, LANES), 1)
    lower = t >= s

    @pl.loop(0, peers)
    def _(k):
        ell = -rates_ref[...] * code_sums(side_ref[k, pl.ds(wide, 16), :])
        ell_col = columns_of(ell)
        b = proj_ref[k, :LANES, :NS]
        c = proj_ref[k, :LANES, NS:]
        gram = dot(c, b, INNER)
        states = [enter_ref[k, pl.ds(pair * NS, NS), :] for pair in range(pairs)]
        carry = carried(jnp.concatenate([c, c], 1), jnp.exp(ell_col), states)
        for pair in range(pairs):
            rows = pl.ds(pair * LANES, LANES)
            mixes = []
            for h in (2 * pair, 2 * pair + 1):
                gap = jnp.where(lower, ell_col[:, h : h + 1] - ell[h : h + 1], -jnp.inf)
                mixes.append((gram * jnp.exp(gap)).astype(BF16))
            x = x_ref[k, rows, :]
            zero = jnp.zeros_like(x)
            right = jnp.concatenate([lane_select(x, zero), lane_select(zero, x)], 0)
            y_ref[k, rows, :] = dot(jnp.concatenate(mixes, 1), right) + carry[pair]
            gate = side_ref[k, rows, :].astype(F32)
            silu_ref[k, rows, :] = gate / (1.0 + jnp.exp(-gate))


def gated_kernel(planes, with_full, y_ref, silu_ref, proj_ref, side_ref, rates_ref, *rest):
    ends, rest = rest[: planes - 1], rest[planes - 1 :]
    out_ref = rest[0]
    count_ref, enter_ref = rest[-2:]
    peers, wide = y_ref.shape[:2]
    pairs = wide // LANES
    rates = rates_ref[...]
    count_ref[...] = jnp.zeros_like(count_ref)
    for pair in range(pairs):
        rows = pl.ds(pair * LANES, LANES)
        state = ends[-1][rows, :].astype(F32)
        for i in range(planes - 3, -1, -1):
            decay = joined_row(ends[i][wide:, :].astype(F32), pair)
            state = ends[i][rows, :].astype(F32) + decay * state
        enter_ref[rows, :] = state

    @pl.loop(0, peers)
    def _(k):
        sums = code_sums(side_ref[k, pl.ds(wide, 16), :])
        grown = columns_of(jnp.exp(-rates * (sums + count_ref[...])))
        count_ref[...] += jnp.broadcast_to(sums[:, LANES - 1 :], count_ref.shape)
        c = proj_ref[k, :LANES, NS:]
        states = [enter_ref[pl.ds(pair * NS, NS), :] for pair in range(pairs)]
        carry = carried(jnp.concatenate([c, c], 1), grown, states)
        for pair in range(pairs):
            rows = pl.ds(pair * LANES, LANES)
            y = (y_ref[k, rows, :] + carry[pair]) * silu_ref[k, rows, :]
            out_ref[k, rows, :] = y.astype(BF16)
            if with_full:
                rest[1][k, rows, :] = y


def finish_kernel(channels, with_proj, g_ref, gain_ref, *rest):
    if with_proj:
        bc_ref, out_ref, proj_ref = rest
    else:
        (out_ref,) = rest
    parts, wide = g_ref.shape[0], g_ref.shape[1] // LANES
    squares = jnp.zeros((LANES, LANES), F32)
    for p in range(parts):
        for i in range(wide):
            g = g_ref[p, i * LANES : (i + 1) * LANES, :].astype(F32)
            squares += g * g
    inverse = 1.0 / jnp.sqrt(jnp.sum(squares, 1, keepdims=True) / channels + EPSILON)
    scaled = jnp.zeros((LANES, LANES), F32)
    proj = jnp.zeros((LANES, 2 * NS), F32)
    for p in range(parts):
        for i in range(wide):
            n = p * wide + i
            g = g_ref[p, i * LANES : (i + 1) * LANES, :].astype(F32)
            out = g * inverse * gain_ref[n : n + 1, :]
            out_ref[:, n * LANES : (n + 1) * LANES] = out
            if with_proj:
                x = out.astype(BF16)
                proj += dot(x, bc_ref[n * LANES : (n + 1) * LANES, :])
                x = x.astype(F32)
                scaled += x * x
    if with_proj:
        mean = jnp.sum(scaled, 1, keepdims=True) / channels
        both = 1.0 / jnp.sqrt(mean + EPSILON)
        proj_ref[:LANES, :] = (proj * both).astype(BF16)
        wide = jnp.broadcast_to(both, (LANES, LANES)).T
        proj_ref[LANES:, :] = split_rows(wide[:1], jnp.broadcast_to(inverse, wide.shape).T[:1])


def params(mib=12):
    return pltpu.CompilerParams(vmem_limit_bytes=mib * MIB)


def cost(flops, nbytes, exps=0):
    return pl.CostEstimate(flops=flops, bytes_accessed=nbytes, transcendentals=exps)


def whole_block(shape):
    return pl.BlockSpec(shape, lambda *_: (0,) * len(shape))


def head_sharded(
    planes, queries, rotated_keys, values, decay_rates, decay_codes, gate_input, norm_gain, bc_weight
):
    tokens, channels = queries.shape
    peers = lax.axis_size("peer")
    wide = channels // peers
    pairs = wide // LANES
    heads = decay_codes.shape[1] // peers
    peer = lax.axis_index("peer")
    place = jnp.stack([lax.axis_index("plane"), peer]).astype(jnp.int32)

    def moved(x, distance):
        return lax.ppermute(x, "plane", [(i, i + distance) for i in range(planes - distance)])

    kv = pl.pallas_call(
        pack_kv_kernel,
        out_shape=jax.ShapeDtypeStruct((peers, 2 * tokens, HEAD_SIZE), BF16),
        compiler_params=params(),
        name="pack_kv",
    )(rotated_keys, values)
    kv_own = lax.all_to_all(kv, "peer", 0, 0)
    with jax.named_scope("shift_near"):
        kv_one = moved(kv_own, 1)
    kv_two = moved(kv_one, 1)

    packed = pl.pallas_call(
        pack_heads_kernel,
        out_shape=jax.ShapeDtypeStruct((peers, wide, LANES), BF16),
        compiler_params=params(),
        name="pack_queries",
    )(queries)
    with jax.named_scope("trade_queries"):
        arrived = lax.all_to_all(packed, "peer", 0, 0)

    arrived, gate_after = lax.optimization_barrier((arrived, gate_input))
    coded = jnp.stack([decay_codes >> 7, decay_codes & 127], 0).astype(BF16)
    coded = jnp.transpose(coded.reshape(2, tokens, peers, heads), (2, 0, 3, 1))
    coded = coded.reshape(peers, 2 * heads, tokens)
    packed = pl.pallas_call(
        pack_heads_kernel,
        out_shape=jax.ShapeDtypeStruct((peers, wide + 16, LANES), BF16),
        compiler_params=params(),
        name="pack_gates",
    )(gate_after, coded)
    with jax.named_scope("trade_gates"):
        side = lax.all_to_all(packed, "peer", 0, 0)

    def keys_spec(which):
        return pl.BlockSpec((peers, tokens, HEAD_SIZE), lambda j, s: (0, which, 0))

    steps = 1

    def block(rows, lanes=LANES):
        return pl.BlockSpec((steps, rows, lanes), lambda j, s: (j, 0, 0))

    proj_rows = tokens + 16
    with jax.named_scope("attention"):
        attended, partial = pl.pallas_call(
            attend_kernel,
            grid_spec=pltpu.PrefetchScalarGridSpec(
                num_scalar_prefetch=1,
                grid=(peers // steps,),
                in_specs=[block(wide)]
                + [keys_spec(0), keys_spec(1)] * 3
                + [pl.BlockSpec((wide, 2 * NS), lambda j, s: (s[1], 0))],
                out_specs=[block(wide), block(tokens + 8, 2 * NS)],
                scratch_shapes=[pltpu.VMEM((peers, 2 * tokens, 2 * tokens), F32)] * 3,
            ),
            out_shape=[
                jax.ShapeDtypeStruct((peers, wide, LANES), BF16),
                jax.ShapeDtypeStruct((peers, tokens + 8, 2 * NS), F32),
            ],
            compiler_params=params(20),
            cost_estimate=cost(5 * 10**9, 4 * 10**6, 9 * 10**6),
            name="attend",
        )(place, arrived, kv_own, kv_own, kv_one, kv_one, kv_two, kv_two, bc_weight)

    partial, side = lax.optimization_barrier((partial, side))
    with jax.named_scope("trade_partial"):
        shares = lax.all_to_all(partial, "peer", 0, 0)
    proj = pl.pallas_call(
        functools.partial(project_kernel, channels),
        in_specs=[whole_block((peers, tokens + 8, 2 * NS))],
        out_specs=whole_block((proj_rows, 2 * NS)),
        out_shape=jax.ShapeDtypeStruct((proj_rows, 2 * NS), BF16),
        name="project",
    )(shares)

    rates = lax.dynamic_slice_in_dim(decay_rates, peer * heads, heads, 0)
    rates = jnp.broadcast_to(rates[:, None], (heads, LANES))
    gains = lax.dynamic_slice_in_dim(norm_gain.reshape(peers, pairs, LANES), peer, 1, 0)[0]
    full_shape = jax.ShapeDtypeStruct((peers, wide, LANES), F32)
    half_shape = jax.ShapeDtypeStruct((peers, wide, LANES), BF16)

    def ssd(x, projected, with_gain):
        operands = [x, projected, side, rates] + ([gains] if with_gain else [])
        normed, entering, end = pl.pallas_call(
            functools.partial(states_kernel, with_gain),
            out_shape=[half_shape, full_shape, jax.ShapeDtypeStruct((wide + 16, LANES), BF16)],
            scratch_shapes=[pltpu.VMEM((wide, LANES), F32), pltpu.VMEM((heads, LANES), F32)],
            compiler_params=params(),
            cost_estimate=cost(10**9, 4 * 10**6),
            name="states",
        )(*operands)
        earlier = [moved(end, i) for i in range(1, planes)]
        y, silu = pl.pallas_call(
            local_kernel,
            out_shape=[full_shape, full_shape],
            compiler_params=params(),
            cost_estimate=cost(2 * 10**9, 5 * 10**6, 10**6),
            name="local",
        )(normed, projected, side, rates, entering)
        return pl.pallas_call(
            functools.partial(gated_kernel, planes, not with_gain),
            out_shape=[half_shape] if with_gain else [half_shape, full_shape],
            scratch_shapes=[pltpu.VMEM((heads, LANES), F32), pltpu.VMEM((wide, LANES), F32)],
            compiler_params=params(),
            cost_estimate=cost(10**9, 5 * 10**6, 10**6),
            name="gated",
        )(y, silu, projected, side, rates, *earlier)

    gain_rows = norm_gain.reshape(channels // LANES, LANES)
    gathered = (peers, wide, LANES)

    projected = lax.all_gather(proj, "peer")
    gated, full = ssd(attended, projected, False)
    first, proj = pl.pallas_call(
        functools.partial(finish_kernel, channels, True),
        in_specs=[
            whole_block(gathered),
            whole_block(gain_rows.shape),
            whole_block((channels, 2 * NS)),
        ],
        out_specs=[whole_block((tokens, channels)), whole_block((proj_rows, 2 * NS))],
        out_shape=[
            jax.ShapeDtypeStruct((tokens, channels), F32),
            jax.ShapeDtypeStruct((proj_rows, 2 * NS), BF16),
        ],
        compiler_params=params(),
        name="finish_first",
    )(lax.all_to_all(gated, "peer", 0, 0), gain_rows, bc_weight)
    projected = lax.all_gather(proj, "peer")
    (gated,) = ssd(full, projected, True)
    second = pl.pallas_call(
        functools.partial(finish_kernel, channels, False),
        in_specs=[whole_block(gathered), whole_block(gain_rows.shape)],
        out_specs=whole_block((tokens, channels)),
        out_shape=jax.ShapeDtypeStruct((tokens, channels), F32),
        compiler_params=params(),
        name="finish_second",
    )(lax.all_to_all(gated, "peer", 0, 0), gain_rows)
    return first, second


def solution(mesh):
    seq, tp = mesh.shape["seq"], mesh.shape["tp"]
    peers = KEY_VALUE_HEADS // tp
    planes = seq // peers
    grouped = (
        tp == 1
        and seq % peers == 0
        and planes >= 3
        and 2 * peers * STRETCH == WINDOW_LENGTH
    )

    def call(*args):
        tokens = args[0].shape[0] // seq
        if grouped and tokens == STRETCH:
            devices = mesh.devices.reshape(planes, peers, tp)
            inner = Mesh(devices, ("plane", "peer", "tp"))
            line, body = ("plane", "peer"), functools.partial(head_sharded, planes)
        else:
            inner, line, body = mesh, "seq", on_device
        split = P(line, "tp")
        return jax.shard_map(
            body,
            mesh=inner,
            in_specs=(split, split, split, P("tp"), split, split, P("tp"), P("tp", None)),
            out_specs=(split, split),
            check_vma=False,
        )(*args)

    return call
```

```python
import functools
import math

import jax
import jax.numpy as jnp
from jax import lax
from jax.experimental import pallas as pl
from jax.experimental.pallas import tpu as pltpu
from jax.sharding import Mesh
from jax.sharding import PartitionSpec as P

QUERY_HEADS = 32
KEY_VALUE_HEADS = 8
HEAD_SIZE = 128
SH = 64
SP = 64
NS = 128
WINDOW_LENGTH = 2048
STRETCH = 128


EPSILON = 1e-05


def shifted(block, axis, distance):
    devices = range(lax.axis_size(axis))
    route = [(i - distance, i) for i in devices if i - distance in devices]
    return lax.ppermute(block, axis, route)


def prefix(x, axis, combine, identity):
    peers, index = (lax.axis_size(axis), lax.axis_index(axis))
    everything = jax.tree.map(lambda part: lax.all_gather(part, axis), x)
    start = jax.tree.map(
        lambda part, zero: jnp.broadcast_to(jnp.asarray(zero, part.dtype), part.shape), x, identity
    )

    def step(k, before):
        reached = k < index
        new = combine(before, jax.tree.map(lambda part: part[k], everything))
        return jax.tree.map(lambda a, b: jnp.where(reached, a, b), new, before)

    return lax.fori_loop(0, peers, step, start)


def combine_states(earlier, later):
    return (earlier[0] * later[0], later[0][..., None, None] * earlier[1] + later[1])


def attention(queries, rotated_keys, values):
    tok_rows = queries.shape[0]
    seq_index = lax.axis_index("seq")
    reach = WINDOW_LENGTH // tok_rows
    kv_local = rotated_keys.shape[1] // HEAD_SIZE
    group_length = QUERY_HEADS // KEY_VALUE_HEADS
    paired = jnp.stack([rotated_keys, values], 0)
    moving = paired
    arrived = []
    for _ in range(reach):
        moving = shifted(moving, "seq", 1)
        arrived.append(moving)
    kv_blocks = arrived[::-1]
    window_kv = jnp.concatenate(kv_blocks + [paired], 1)
    grouped = queries.reshape(tok_rows, kv_local, group_length, HEAD_SIZE)
    score_scale = 1.0 / math.sqrt(HEAD_SIZE)
    query_pos = seq_index * tok_rows + jnp.arange(tok_rows, dtype=jnp.int32)
    base_pos = (seq_index - reach) * tok_rows

    def block_scores(key_block):
        key_row_block = lax.dynamic_slice_in_dim(
            window_kv[0], key_block * tok_rows, tok_rows, 0
        ).reshape(tok_rows, kv_local, HEAD_SIZE)
        scores = (
            jnp.einsum("tkgd,skd->kgts", grouped, key_row_block, preferred_element_type=jnp.float32)
            * score_scale
        )
        key_pos = base_pos + key_block * tok_rows + jnp.arange(tok_rows, dtype=jnp.int32)
        allowed = (
            (key_pos[None, :] <= query_pos[:, None])
            & (key_pos[None, :] > query_pos[:, None] - WINDOW_LENGTH)
            & (key_pos[None, :] >= 0)
        )
        return jnp.where(allowed[None, None], scores, -jnp.inf)

    def visit_order(counter):
        return (counter + reach) % (reach + 1)

    def totals(counter, running):
        row_max, row_sum = running
        scores = block_scores(visit_order(counter))
        new_max = jnp.maximum(row_max, jnp.max(scores, axis=3))
        rescale = jnp.exp(row_max - new_max)
        row_sum = row_sum * rescale + jnp.sum(jnp.exp(scores - new_max[..., None]), axis=3)
        return (new_max, row_sum)

    max_init = jnp.full((kv_local, group_length, tok_rows), -jnp.inf, jnp.float32)
    row_max, row_sum = lax.fori_loop(0, reach + 1, totals, (max_init, jnp.zeros_like(max_init)))

    def weighted(counter, accumulated):
        key_block = visit_order(counter)
        scores = block_scores(key_block)
        value_row_block = lax.dynamic_slice_in_dim(
            window_kv[1], key_block * tok_rows, tok_rows, 0
        ).reshape(tok_rows, kv_local, HEAD_SIZE)
        probs = (jnp.exp(scores - row_max[..., None]) / row_sum[..., None]).astype(jnp.bfloat16)
        return accumulated + jnp.einsum(
            "kgts,skd->kgtd", probs, value_row_block, preferred_element_type=jnp.float32
        )

    acc_init = jnp.zeros((kv_local, group_length, tok_rows, HEAD_SIZE), jnp.float32)
    accumulated = lax.fori_loop(0, reach + 1, weighted, acc_init)
    mixed_rows = jnp.transpose(accumulated, (2, 0, 1, 3))
    return mixed_rows.astype(jnp.bfloat16).reshape(tok_rows, kv_local * group_length * HEAD_SIZE)


def core(inputs, decay_rates, decay_codes, gate_input, norm_gain, bc_weight):
    tok_rows = inputs.shape[0]
    head_count = decay_rates.shape[0]
    channels = SH * SP
    as_float = inputs.astype(jnp.float32)
    own_squares = jnp.sum(as_float * as_float, axis=1)
    partial_value = jnp.dot(inputs, bc_weight, preferred_element_type=jnp.float32)
    total_squares = lax.psum(own_squares, "tp")
    spread = jnp.sqrt(total_squares / channels + EPSILON)[:, None]
    projected = lax.psum(partial_value / spread, "tp")
    normed = (as_float / spread).astype(jnp.bfloat16)
    projected = projected.astype(jnp.bfloat16)
    stretch_count = tok_rows // STRETCH
    x_stretches = normed.reshape(stretch_count, STRETCH, head_count, SP)
    b_stretches = projected[:, :NS].reshape(stretch_count, STRETCH, NS)
    c_stretches = projected[:, NS:].reshape(stretch_count, STRETCH, NS)
    summed_codes = jnp.cumsum(
        decay_codes.reshape(stretch_count, STRETCH, head_count), axis=1, dtype=jnp.int32
    )
    log_decay = -decay_rates * summed_codes.astype(jnp.float32)
    decay_by_head = jnp.transpose(log_decay, (0, 2, 1))
    gram_matrix = jnp.einsum(
        "ctn,csn->cts", c_stretches, b_stretches, preferred_element_type=jnp.float32
    )
    lower_mask = jnp.arange(STRETCH)[:, None] >= jnp.arange(STRETCH)[None, :]
    decay_gaps = jnp.where(
        lower_mask, decay_by_head[..., :, None] - decay_by_head[..., None, :], 0.0
    )
    mixing = jnp.where(lower_mask, gram_matrix[:, None] * jnp.exp(decay_gaps), 0.0).astype(
        jnp.bfloat16
    )
    y_local = jnp.einsum("chts,cshp->cthp", mixing, x_stretches, preferred_element_type=jnp.float32)
    tail_decay = jnp.exp(decay_by_head[..., -1:] - decay_by_head)
    b_weighted = (b_stretches.astype(jnp.float32)[:, None] * tail_decay[..., None]).astype(
        jnp.bfloat16
    )
    contrib = jnp.einsum(
        "chsn,cshp->chnp", b_weighted, x_stretches, preferred_element_type=jnp.float32
    )
    stretch_decay = jnp.exp(decay_by_head[..., -1])
    carried_decay = jnp.ones((head_count,), jnp.float32)
    carried_state = jnp.zeros((head_count, NS, SP), jnp.float32)
    carried_state = stretch_decay[0][:, None, None] * carried_state + contrib[0]
    carried_decay = carried_decay * stretch_decay[0]
    _, entering = prefix(
        (carried_decay, carried_state),
        "seq",
        combine_states,
        (jnp.ones_like(carried_decay), jnp.zeros_like(carried_state)),
    )
    states = [entering]
    stacked = jnp.stack(states, 0)
    c_weighted = c_stretches.astype(jnp.float32)[:, None] * jnp.exp(decay_by_head)[..., None]
    y_carried = jnp.einsum(
        "chtn,chnp->cthp",
        c_weighted,
        stacked,
        precision=lax.Precision.HIGHEST,
        preferred_element_type=jnp.float32,
    )
    outputs = (y_local + y_carried).reshape(tok_rows, head_count * SP)
    gated_out = outputs * jax.nn.silu(gate_input.astype(jnp.float32))
    gate_squares = lax.psum(jnp.sum(gated_out * gated_out, axis=1), "tp")
    out_scale = jnp.sqrt(gate_squares / channels + EPSILON)[:, None]
    return gated_out / out_scale * norm_gain


def on_device(
    queries, rotated_keys, values, decay_rates, decay_codes, gate_input, norm_gain, bc_weight
):
    attended = attention(queries, rotated_keys, values)
    first_pass = core(attended, decay_rates, decay_codes, gate_input, norm_gain, bc_weight)
    pass_input = first_pass.astype(jnp.bfloat16)
    second_pass = core(pass_input, decay_rates, decay_codes, gate_input, norm_gain, bc_weight)
    return (first_pass, second_pass)


F32 = jnp.float32
BF16 = jnp.bfloat16
LANES = 128
INNER = (((1,), (1,)), ((), ()))
MIB = 1024 * 1024


def dot(a, b, dims=(((1,), (0,)), ((), ()))):
    return lax.dot_general(a, b, dims, preferred_element_type=F32)


def lane_select(low, high):
    lane = lax.broadcasted_iota(jnp.int32, (1, LANES), 1)
    return jnp.where(lane < SP, low, high)


def split_rows(*rows):
    which = lax.broadcasted_iota(jnp.int32, (16, LANES), 0)
    tile = jnp.zeros((16, LANES), F32)
    for i, row in enumerate(rows):
        for n in range(3):
            piece = row.astype(BF16).astype(F32)
            tile = jnp.where(which == 3 * i + n, piece, tile)
            row = row - piece
    return jnp.concatenate([tile, jnp.zeros_like(tile)], 1).astype(BF16)


def joined_row(pieces, i):
    return pieces[3 * i : 3 * i + 1] + pieces[3 * i + 1 : 3 * i + 2] + pieces[3 * i + 2 : 3 * i + 3]


def column(row):
    return jnp.broadcast_to(row, (LANES, LANES)).T


def pack_kv_kernel(k_ref, v_ref, out_ref):
    for p in range(out_ref.shape[0]):
        cols = pl.ds(p * LANES, LANES)
        out_ref[p, :LANES, :] = k_ref[:, cols]
        out_ref[p, LANES:, :] = v_ref[:, cols]


def pack_heads_kernel(x_ref, *rest):
    out_ref = rest[-1]
    peers = out_ref.shape[0]
    heads = x_ref.shape[1] // LANES // peers
    for p in range(peers):
        for h in range(heads):
            cols = pl.ds((p * heads + h) * LANES, LANES)
            out_ref[p, pl.ds(h * LANES, LANES), :] = x_ref[:, cols]
        if len(rest) == 3:
            out_ref[p, pl.ds(heads * LANES, 16), :] = rest[0][p]


def same_kernel(x_ref, after_ref, out_ref):
    pass


def after(x, earlier):
    anywhere = pl.BlockSpec(memory_space=pl.ANY)
    return pl.pallas_call(
        same_kernel,
        in_specs=[anywhere, pl.BlockSpec(memory_space=pltpu.VMEM)],
        out_specs=anywhere,
        out_shape=jax.ShapeDtypeStruct(x.shape, x.dtype),
        input_output_aliases={0: 0},
        name="after",
    )(x, earlier)


def attend_kernel(
    place_ref, q_ref, ko_ref, vo_ref, k1_ref, v1_ref, k2_ref, v2_ref, bc_ref, x_ref, part_ref, *scores
):
    plane = place_ref[0]
    blocks = ko_ref.shape[0]
    steps, rows = q_ref.shape[:2]
    half = blocks // 2
    count = 2 * half
    unit_rows = 2 * LANES
    splits = rows // unit_rows
    factor = math.log2(math.e) / math.sqrt(HEAD_SIZE)
    bias2 = jnp.where(plane >= 2, 0.0, -jnp.inf).astype(F32)
    lane = lax.broadcasted_iota(jnp.int32, (1, 2 * LANES), 1)
    t_pos = lax.broadcasted_iota(jnp.int32, (unit_rows, LANES), 0) % LANES
    s_pos = lax.broadcasted_iota(jnp.int32, (unit_rows, LANES), 1)
    causal = s_pos <= t_pos

    def unit(n):
        here, part = n // splits, n % splits
        j = pl.program_id(0) * steps + here
        s_ref = scores[n % len(scores)]
        span = pl.ds(part * unit_rows, unit_rows)
        held = {}

        def mixed(i, own_ref, far_ref):
            return jnp.where(i < j, own_ref[i], far_ref[i + 1])

        def score(i):
            q = q_ref[here, span, :]
            if i < half:
                s = dot(q, k1_ref[2 * i : 2 * i + 2].reshape(2 * LANES, HEAD_SIZE), INNER)
                key = "near"
            else:
                a = 2 * (i - half)
                first = mixed(a, ko_ref, k2_ref)
                bias_a = jnp.where(a < j, 0.0, bias2)
                if i < count - 1:
                    bias_b = jnp.where(a + 1 < j, 0.0, bias2)
                    s = dot(q, jnp.concatenate([first, mixed(a + 1, ko_ref, k2_ref)], 0), INNER)
                    s = s + jnp.where(lane < LANES, bias_a, bias_b)
                else:
                    s = dot(q, jnp.concatenate([first, ko_ref[j]], 0), INNER)
                    edge = dot(q, k2_ref[j], INNER) + bias2
                    s = jnp.concatenate(
                        [s[:, :LANES] + bias_a, jnp.where(causal, s[:, LANES:], edge)], 1
                    )
                key = "rest"
            s_ref[i] = s
            high = jnp.maximum(s[:, :LANES], s[:, LANES:])
            held[key] = jnp.maximum(held[key], high) if key in held else high
            if i == count - 1:
                near = jnp.where(plane >= 1, held.pop("near"), -jnp.inf)
                top = jnp.max(jnp.maximum(near, held.pop("rest")), axis=1, keepdims=True) * factor
                held["top"] = top
                held["top_near"] = jnp.where(plane >= 1, top, jnp.inf)

        def weigh(i):
            p = jnp.exp2(s_ref[i] * factor - held["top_near" if i < half else "top"])
            s_ref[i] = p
            both = p[:, :LANES] + p[:, LANES:]
            held["sum"] = held["sum"] + both if "sum" in held else both
            if i == count - 1:
                held["inverse"] = 1.0 / jnp.sum(held.pop("sum"), axis=1, keepdims=True)

        def mix(i):
            p = (s_ref[i] * held["inverse"]).astype(BF16)
            if i < half:
                vals = v1_ref[2 * i : 2 * i + 2].reshape(2 * LANES, HEAD_SIZE)
            else:
                a = 2 * (i - half)
                first = mixed(a, vo_ref, v2_ref)
                if i < count - 1:
                    vals = jnp.concatenate([first, mixed(a + 1, vo_ref, v2_ref)], 0)
                else:
                    last = p[:, LANES:]
                    zero = jnp.zeros_like(last)
                    far = jnp.where(causal, zero, last)
                    p = jnp.concatenate([p[:, :LANES], jnp.where(causal, last, zero)], 1)
                    vals = jnp.concatenate([first, vo_ref[j]], 0)
                    held["total"] += dot(far, v2_ref[j])
            new = dot(p, vals)
            held["total"] = held["total"] + new if "total" in held else new
            if i == count - 1:
                x_ref[here, span, :] = held.pop("total").astype(BF16)

        return score, weigh, mix

    units = [unit(n) for n in range(steps * splits)]
    for phase in range(len(units) + 2):
        for i in range(count):
            for stage in (2, 1, 0):
                n = phase - stage
                if 0 <= n < len(units):
                    units[n][stage](i)
    for here in range(steps):
        part = jnp.zeros((LANES, 2 * NS), F32)
        squares = jnp.zeros((LANES, LANES), F32)
        for h in range(rows // LANES):
            piece = x_ref[here, pl.ds(h * LANES, LANES), :]
            part += dot(piece, bc_ref[pl.ds(h * LANES, LANES), :])
            wide = piece.astype(F32)
            squares += wide * wide
        high = squares.astype(BF16)
        low = (squares - high.astype(F32)).astype(BF16)
        row_ones = jnp.ones((16, LANES), BF16)
        row = dot(row_ones, high, INNER) + dot(row_ones, low, INNER)
        part_ref[here, :LANES, :] = part
        part_ref[here, LANES:, :LANES] = row[:8]
        part_ref[here, LANES:, LANES:] = jnp.zeros_like(row[:8])


def project_kernel(channels, part_ref, out_ref):
    total = part_ref[0]
    for i in range(1, part_ref.shape[0]):
        total += part_ref[i]
    inverse = 1.0 / jnp.sqrt(total[LANES : LANES + 1, :LANES] / channels + EPSILON)
    scale = column(inverse)
    out_ref[:LANES, :NS] = (total[:LANES, :NS] * scale).astype(BF16)
    out_ref[:LANES, NS:] = (total[:LANES, NS:] * scale).astype(BF16)
    out_ref[LANES:, :] = split_rows(inverse)


def code_sums(codes):
    u = lax.broadcasted_iota(jnp.int32, (LANES, LANES), 0)
    t = lax.broadcasted_iota(jnp.int32, (LANES, LANES), 1)
    upper = jnp.where(u <= t, 1.0, 0.0).astype(BF16)
    sums = dot(codes, upper)
    return sums[:8] * 128.0 + sums[8:]


def columns_of(by_row):
    pad = jnp.zeros((LANES - by_row.shape[0], LANES), F32)
    return jnp.concatenate([by_row, pad], 0).T


def states_kernel(with_gain, x_ref, proj_ref, side_ref, rates_ref, *rest):
    if with_gain:
        gain_ref, *rest = rest
    normed_ref, enter_ref, end_ref, state_ref, count_ref = rest
    peers, wide = x_ref.shape[:2]
    pairs = wide // LANES
    rates = rates_ref[...]
    state_ref[...] = jnp.zeros_like(state_ref)
    count_ref[...] = jnp.zeros_like(count_ref)

    @pl.loop(0, peers)
    def _(k):
        sums = code_sums(side_ref[k, pl.ds(wide, 16), :])
        last = sums[:, LANES - 1 :]
        weights = jnp.exp(-rates * (last - sums))
        block_decay = jnp.exp(-rates * last)
        count_ref[...] += jnp.broadcast_to(last, count_ref.shape)
        b_across = proj_ref[k, :LANES, :NS].astype(F32).T
        pieces = proj_ref[k, LANES:, :LANES].astype(F32)
        inverse = column(joined_row(pieces, 0))
        if with_gain:
            out_inverse = column(joined_row(pieces, 1))
        for pair in range(pairs):
            rows = pl.ds(pair * LANES, LANES)
            x = x_ref[k, rows, :].astype(F32)
            if with_gain:
                x = x * out_inverse * gain_ref[pair : pair + 1, :]
                x = x.astype(BF16).astype(F32)
            x = (x * inverse).astype(BF16)
            normed_ref[k, rows, :] = x
            h = 2 * pair
            b = jnp.concatenate(
                [b_across * weights[h : h + 1], b_across * weights[h + 1 : h + 2]], 0
            ).astype(BF16)
            both = dot(b, x)
            contrib = lane_select(both[:NS], both[NS:])
            state = state_ref[rows, :]
            enter_ref[k, rows, :] = state
            decay = lane_select(block_decay[h : h + 1], block_decay[h + 1 : h + 2])
            state_ref[rows, :] = decay * state + contrib

    end_ref[:wide, :] = state_ref[...].astype(BF16)
    whole = jnp.exp(-rates * count_ref[...])
    which = lax.broadcasted_iota(jnp.int32, (16, LANES), 0)
    tile = jnp.zeros((16, LANES), F32)
    for pair in range(pairs):
        row = lane_select(whole[2 * pair : 2 * pair + 1], whole[2 * pair + 1 : 2 * pair + 2])
        for n in range(3):
            piece = row.astype(BF16).astype(F32)
            tile = jnp.where(which == 3 * pair + n, piece, tile)
            row = row - piece
    end_ref[wide:, :] = tile.astype(BF16)


def carried(c_twice, grown, states):
    parts = []
    for state in states:
        high = state.astype(BF16)
        low = (state - high.astype(F32)).astype(BF16)
        parts.append(jnp.concatenate([high, low], 0))
    out = dot(c_twice, jnp.concatenate(parts, 1))
    scaled = []
    for pair in range(len(states)):
        scale = lane_select(grown[:, 2 * pair : 2 * pair + 1], grown[:, 2 * pair + 1 : 2 * pair + 2])
        scaled.append(scale * out[:, pair * LANES : (pair + 1) * LANES])
    return scaled


def local_kernel(x_ref, proj_ref, side_ref, rates_ref, enter_ref, y_ref, silu_ref):
    peers, wide = x_ref.shape[:2]
    pairs = wide // LANES
    t = lax.broadcasted_iota(jnp.int32, (LANES, LANES), 0)
    s = lax.broadcasted_iota(jnp.int32, (LANES, LANES), 1)
    lower = t >= s

    @pl.loop(0, peers)
    def _(k):
        ell = -rates_ref[...] * code_sums(side_ref[k, pl.ds(wide, 16), :])
        ell_col = columns_of(ell)
        b = proj_ref[k, :LANES, :NS]
        c = proj_ref[k, :LANES, NS:]
        gram = dot(c, b, INNER)
        states = [enter_ref[k, pl.ds(pair * NS, NS), :] for pair in range(pairs)]
        carry = carried(jnp.concatenate([c, c], 1), jnp.exp(ell_col), states)
        for pair in range(pairs):
            rows = pl.ds(pair * LANES, LANES)
            mixes = []
            for h in (2 * pair, 2 * pair + 1):
                gap = jnp.where(lower, ell_col[:, h : h + 1] - ell[h : h + 1], -jnp.inf)
                mixes.append((gram * jnp.exp(gap)).astype(BF16))
            x = x_ref[k, rows, :]
            zero = jnp.zeros_like(x)
            right = jnp.concatenate([lane_select(x, zero), lane_select(zero, x)], 0)
            y_ref[k, rows, :] = dot(jnp.concatenate(mixes, 1), right) + carry[pair]
            gate = side_ref[k, rows, :].astype(F32)
            silu_ref[k, rows, :] = gate / (1.0 + jnp.exp(-gate))


def gated_kernel(planes, with_full, y_ref, silu_ref, proj_ref, side_ref, rates_ref, *rest):
    ends, rest = rest[: planes - 1], rest[planes - 1 :]
    out_ref = rest[0]
    count_ref, enter_ref = rest[-2:]
    peers, wide = y_ref.shape[:2]
    pairs = wide // LANES
    rates = rates_ref[...]
    count_ref[...] = jnp.zeros_like(count_ref)
    for pair in range(pairs):
        rows = pl.ds(pair * LANES, LANES)
        state = ends[-1][rows, :].astype(F32)
        for i in range(planes - 3, -1, -1):
            decay = joined_row(ends[i][wide:, :].astype(F32), pair)
            state = ends[i][rows, :].astype(F32) + decay * state
        enter_ref[rows, :] = state

    @pl.loop(0, peers)
    def _(k):
        sums = code_sums(side_ref[k, pl.ds(wide, 16), :])
        grown = columns_of(jnp.exp(-rates * (sums + count_ref[...])))
        count_ref[...] += jnp.broadcast_to(sums[:, LANES - 1 :], count_ref.shape)
        c = proj_ref[k, :LANES, NS:]
        states = [enter_ref[pl.ds(pair * NS, NS), :] for pair in range(pairs)]
        carry = carried(jnp.concatenate([c, c], 1), grown, states)
        for pair in range(pairs):
            rows = pl.ds(pair * LANES, LANES)
            y = (y_ref[k, rows, :] + carry[pair]) * silu_ref[k, rows, :]
            out_ref[k, rows, :] = y.astype(BF16)
            if with_full:
                rest[1][k, rows, :] = y


def finish_kernel(channels, with_proj, g_ref, gain_ref, *rest):
    if with_proj:
        bc_hbm, out_ref, proj_ref, bc_ref, bc_sem = rest
        fetch = pltpu.make_async_copy(bc_hbm, bc_ref, bc_sem)
        fetch.start()
    else:
        (out_ref,) = rest
    parts, wide = g_ref.shape[0], g_ref.shape[1] // LANES
    squares = jnp.zeros((LANES, LANES), F32)
    for p in range(parts):
        for i in range(wide):
            g = g_ref[p, i * LANES : (i + 1) * LANES, :].astype(F32)
            squares += g * g
    inverse = 1.0 / jnp.sqrt(jnp.sum(squares, 1, keepdims=True) / channels + EPSILON)
    if with_proj:
        fetch.wait()
    scaled = jnp.zeros((LANES, LANES), F32)
    proj = jnp.zeros((LANES, 2 * NS), F32)
    for p in range(parts):
        for i in range(wide):
            n = p * wide + i
            g = g_ref[p, i * LANES : (i + 1) * LANES, :].astype(F32)
            out = g * inverse * gain_ref[n : n + 1, :]
            out_ref[:, n * LANES : (n + 1) * LANES] = out
            if with_proj:
                x = out.astype(BF16)
                proj += dot(x, bc_ref[n * LANES : (n + 1) * LANES, :])
                x = x.astype(F32)
                scaled += x * x
    if with_proj:
        mean = jnp.sum(scaled, 1, keepdims=True) / channels
        both = 1.0 / jnp.sqrt(mean + EPSILON)
        proj_ref[:LANES, :] = (proj * both).astype(BF16)
        wide = jnp.broadcast_to(both, (LANES, LANES)).T
        proj_ref[LANES:, :] = split_rows(wide[:1], jnp.broadcast_to(inverse, wide.shape).T[:1])


def params(mib=12):
    return pltpu.CompilerParams(vmem_limit_bytes=mib * MIB)


def cost(flops, nbytes, exps=0):
    return pl.CostEstimate(flops=flops, bytes_accessed=nbytes, transcendentals=exps)


def whole_block(shape):
    return pl.BlockSpec(shape, lambda *_: (0,) * len(shape))


def head_sharded(
    planes, queries, rotated_keys, values, decay_rates, decay_codes, gate_input, norm_gain, bc_weight
):
    tokens, channels = queries.shape
    bc_weight = pltpu.with_memory_space_constraint(bc_weight, pltpu.HBM)
    peers = lax.axis_size("peer")
    wide = channels // peers
    pairs = wide // LANES
    heads = decay_codes.shape[1] // peers
    peer = lax.axis_index("peer")
    place = jnp.stack([lax.axis_index("plane"), peer]).astype(jnp.int32)

    def moved(x, distance):
        return lax.ppermute(x, "plane", [(i, i + distance) for i in range(planes - distance)])

    kv = pl.pallas_call(
        pack_kv_kernel,
        out_shape=jax.ShapeDtypeStruct((peers, 2 * tokens, HEAD_SIZE), BF16),
        compiler_params=params(),
        name="pack_kv",
    )(rotated_keys, values)
    kv_own = lax.all_to_all(kv, "peer", 0, 0)
    kv_one = moved(kv_own, 1)
    kv_two = moved(kv_one, 1)

    packed = pl.pallas_call(
        pack_heads_kernel,
        out_shape=jax.ShapeDtypeStruct((peers, wide, LANES), BF16),
        compiler_params=params(),
        in_specs=[pl.BlockSpec(memory_space=pltpu.VMEM), pl.BlockSpec(memory_space=pl.ANY)],
        cost_estimate=cost(2 * 10**10, 2 * 10**6),
        name="pack_queries",
    )(queries, kv_own)
    arrived = lax.all_to_all(packed, "peer", 0, 0)

    coded = jnp.stack([decay_codes >> 7, decay_codes & 127], 0).astype(BF16)
    coded = jnp.transpose(coded.reshape(2, tokens, peers, heads), (2, 0, 3, 1))
    coded = coded.reshape(peers, 2 * heads, tokens)
    packed = pl.pallas_call(
        pack_heads_kernel,
        out_shape=jax.ShapeDtypeStruct((peers, wide + 16, LANES), BF16),
        compiler_params=params(),
        in_specs=[pl.BlockSpec(memory_space=pltpu.VMEM)] * 2 + [pl.BlockSpec(memory_space=pl.ANY)],
        name="pack_gates",
    )(gate_input, coded, arrived)
    side = lax.all_to_all(packed, "peer", 0, 0)

    def keys_spec(which):
        return pl.BlockSpec((peers, tokens, HEAD_SIZE), lambda j, s: (0, which, 0))

    steps = 1

    def block(rows, lanes=LANES):
        return pl.BlockSpec((steps, rows, lanes), lambda j, s: (j, 0, 0))

    proj_rows = tokens + 16
    attended, partial = pl.pallas_call(
        attend_kernel,
        grid_spec=pltpu.PrefetchScalarGridSpec(
            num_scalar_prefetch=1,
            grid=(peers // steps,),
            in_specs=[block(wide)]
            + [keys_spec(0), keys_spec(1)] * 3
            + [pl.BlockSpec((wide, 2 * NS), lambda j, s: (s[1], 0))],
            out_specs=[block(wide), block(tokens + 8, 2 * NS)],
            scratch_shapes=[pltpu.VMEM((peers, 2 * tokens, 2 * tokens), F32)] * 3,
        ),
        out_shape=[
            pltpu.HBM((peers, wide, LANES), BF16),
            pltpu.HBM((peers, tokens + 8, 2 * NS), F32),
        ],
        compiler_params=params(20),
        cost_estimate=cost(5 * 10**9, 4 * 10**6, 9 * 10**6),
        name="attend",
    )(place, arrived, kv_own, kv_own, kv_one, kv_one, kv_two, kv_two, bc_weight)

    partial = after(partial, side[:1, :16])
    shares = lax.all_to_all(partial, "peer", 0, 0)
    proj = pl.pallas_call(
        functools.partial(project_kernel, channels),
        in_specs=[whole_block((peers, tokens + 8, 2 * NS))],
        out_specs=whole_block((proj_rows, 2 * NS)),
        out_shape=jax.ShapeDtypeStruct((proj_rows, 2 * NS), BF16),
        name="project",
    )(shares)

    rates = lax.dynamic_slice_in_dim(decay_rates, peer * heads, heads, 0)
    rates = jnp.broadcast_to(rates[:, None], (heads, LANES))
    gains = lax.dynamic_slice_in_dim(norm_gain.reshape(peers, pairs, LANES), peer, 1, 0)[0]
    full_shape = jax.ShapeDtypeStruct((peers, wide, LANES), F32)
    half_shape = jax.ShapeDtypeStruct((peers, wide, LANES), BF16)

    def ssd(x, projected, with_gain):
        operands = [x, projected, side, rates] + ([gains] if with_gain else [])
        normed, entering, end = pl.pallas_call(
            functools.partial(states_kernel, with_gain),
            out_shape=[half_shape, full_shape, jax.ShapeDtypeStruct((wide + 16, LANES), BF16)],
            scratch_shapes=[pltpu.VMEM((wide, LANES), F32), pltpu.VMEM((heads, LANES), F32)],
            compiler_params=params(),
            cost_estimate=cost(10**9, 4 * 10**6),
            name="states",
        )(*operands)
        earlier = [moved(end, i) for i in range(1, planes)]
        y, silu = pl.pallas_call(
            local_kernel,
            out_shape=[full_shape, full_shape],
            compiler_params=params(),
            cost_estimate=cost(2 * 10**9, 5 * 10**6, 10**6),
            name="local",
        )(normed, projected, side, rates, entering)
        return pl.pallas_call(
            functools.partial(gated_kernel, planes, not with_gain),
            out_shape=[half_shape] if with_gain else [half_shape, pltpu.HBM(full_shape.shape, F32)],
            scratch_shapes=[pltpu.VMEM((heads, LANES), F32), pltpu.VMEM((wide, LANES), F32)],
            compiler_params=params(),
            cost_estimate=cost(10**9, 5 * 10**6, 10**6),
            name="gated",
        )(y, silu, projected, side, rates, *earlier)

    gain_rows = norm_gain.reshape(channels // LANES, LANES)
    gathered = (peers, wide, LANES)

    projected = lax.all_gather(proj, "peer")
    gated, full = ssd(attended, projected, False)
    first, proj = pl.pallas_call(
        functools.partial(finish_kernel, channels, True),
        in_specs=[
            whole_block(gathered),
            whole_block(gain_rows.shape),
            pl.BlockSpec(memory_space=pltpu.HBM),
        ],
        out_specs=[whole_block((tokens, channels)), whole_block((proj_rows, 2 * NS))],
        out_shape=[
            jax.ShapeDtypeStruct((tokens, channels), F32),
            jax.ShapeDtypeStruct((proj_rows, 2 * NS), BF16),
        ],
        scratch_shapes=[pltpu.VMEM((channels, 2 * NS), BF16), pltpu.SemaphoreType.DMA],
        compiler_params=params(),
        name="finish_first",
    )(lax.all_to_all(gated, "peer", 0, 0), gain_rows, bc_weight)
    projected = lax.all_gather(proj, "peer")
    (gated,) = ssd(full, projected, True)
    second = pl.pallas_call(
        functools.partial(finish_kernel, channels, False),
        in_specs=[whole_block(gathered), whole_block(gain_rows.shape)],
        out_specs=whole_block((tokens, channels)),
        out_shape=jax.ShapeDtypeStruct((tokens, channels), F32),
        compiler_params=params(),
        name="finish_second",
    )(lax.all_to_all(gated, "peer", 0, 0), gain_rows)
    return first, second


def solution(mesh):
    seq, tp = mesh.shape["seq"], mesh.shape["tp"]
    peers = KEY_VALUE_HEADS // tp
    planes = seq // peers
    grouped = (
        tp == 1
        and seq % peers == 0
        and planes >= 3
        and 2 * peers * STRETCH == WINDOW_LENGTH
    )

    def call(*args):
        tokens = args[0].shape[0] // seq
        if grouped and tokens == STRETCH:
            devices = mesh.devices.reshape(planes, peers, tp)
            inner = Mesh(devices, ("plane", "peer", "tp"))
            line, body = ("plane", "peer"), functools.partial(head_sharded, planes)
        else:
            inner, line, body = mesh, "seq", on_device
        split = P(line, "tp")
        run = jax.shard_map(
            body,
            mesh=inner,
            in_specs=(split, split, split, P("tp"), split, split, P("tp"), P("tp", None)),
            out_specs=(split, split),
            check_vma=False,
        )
        return run(*args)

    return call
```
